32 devices in a mesh: mem: 4 (over y, x), lat: 8 (over z, core).
Axes of the slice: x: 2, y: 2, z: 4, core: 2. Of those that a mesh axis runs over, the one named last changes fastest.
Arguments:
- gradient: float32 [2, 4, 192, 256], P(None, 'mem', 'lat'), may hold values from -24 to 24
- perturbations: bfloat16 [16, 2, 4, 192, 256], P('mem', None, None, 'lat'), may hold values from -6 to 6
- weights: float32 [16, 4, 192, 256], P('mem', None, 'lat'), may hold values from -6 to 6
- lon_taps: float32 [25], replicated, may hold values from 0.05 to 0.3
- lat_taps: float32 [25], replicated, may hold values from 0.05 to 0.3
- lev_taps: float32 [5], replicated, may hold values from 0.2 to 0.7
- level_order: int32 [4], replicated, may hold values from 0 to 3, each once
Outputs:
- updated_weights: float32 [16, 4, 192, 256], P('mem', None, 'lat')
- increment: float32 [2, 4, 192, 256], P(None, 'mem', 'lat')
The draws below stay inside these ranges and needn't reach their ends.
Inputs may be any that keep to these rules, and one draw needn't show every extreme that they name: `level_order`: each level appears in exactly one slot.
All inputs are finite; a program needn't handle non-finite values.
Results may differ from the reference program's by a relative error of at most 0.0003.
Values sent between devices are 32-bit elements; how exact they have to be, the bound alone decides.
A program may use at most 128 MiB of HBM per device.

```python
import math
import jax
import jax.numpy as jnp
from jax import lax

NLON = 256
MEMBERS = 16
NLEV = 4
NLAT = 192
TAPS = 25
LEV_TAPS = 5


def block_levels(stream_key, dims, pieces, low, top_value):
    level = 1.0
    for dim, shards_of in pieces:
        draws = jax.random.uniform(jax.random.fold_in(jax.random.fold_in(stream_key, 6), dim), (shards_of,), jnp.float32, low / len(pieces), top_value / len(pieces))
        level = level * jnp.repeat(jnp.exp(draws), dims[dim] // shards_of).reshape((-1,) + (1,) * (len(dims) - 1 - dim))
    return level


def noise(key, shape, scale, most, cuts=(), kind=jnp.bfloat16):
    entries = scale * jax.random.normal(key, shape, jnp.float32)
    if cuts:
        entries = entries * block_levels(key, shape, cuts, -0.22, 0.18)
    return jnp.clip(entries, -most, most).astype(kind)


def setup_inputs(seed: int = 0) -> dict:
    arg_keys = jax.random.split(jax.random.key(seed), 8)
    return {
        "gradient": noise(arg_keys[0], (2, NLEV, NLAT, NLON), 4.0, 24.0, ((1, 4), (2, 8)), jnp.float32),
        "perturbations": noise(arg_keys[1], (MEMBERS, 2, NLEV, NLAT, NLON), 1.0, 6.0, ((0, 4), (3, 8))),
        "weights": noise(arg_keys[2], (MEMBERS, NLEV, NLAT, NLON), 1.0, 6.0, ((0, 4), (2, 8)), jnp.float32),
        "lon_taps": jnp.clip(jax.random.uniform(arg_keys[3], (TAPS,), jnp.float32, 0.05, 0.3), 0.05, 0.3),
        "lat_taps": jnp.clip(jax.random.uniform(arg_keys[4], (TAPS,), jnp.float32, 0.05, 0.3), 0.05, 0.3),
        "lev_taps": jnp.clip(jax.random.uniform(arg_keys[5], (LEV_TAPS,), jnp.float32, 0.2, 0.7), 0.2, 0.7),
        "level_order": jax.random.permutation(arg_keys[6], NLEV).astype(jnp.int32),
    }


STEP_RATE = 0.5

def lon_forward(values, tap_weights):
    radius = tap_weights.shape[0] // 2
    result = jnp.zeros_like(values)
    for position in range(tap_weights.shape[0]):
        result = result + tap_weights[position] * jnp.roll(values, radius - position, axis=-1)
    return result

def lon_adjoint(values, tap_weights):
    radius = tap_weights.shape[0] // 2
    result = jnp.zeros_like(values)
    for position in range(tap_weights.shape[0]):
        result = result + tap_weights[position] * jnp.roll(values, position - radius, axis=-1)
    return result

def lat_forward(extended, tap_weights):
    width = tap_weights.shape[0]
    out_rows = extended.shape[-2] - width + 1
    result = tap_weights[0] * lax.slice_in_dim(extended, 0, out_rows, axis=extended.ndim - 2)
    for position in range(1, width):
        result = result + tap_weights[position] * lax.slice_in_dim(extended, position, position + out_rows, axis=extended.ndim - 2)
    return result

def lat_adjoint(extended, tap_weights):
    width = tap_weights.shape[0]
    out_rows = extended.shape[-2] - width + 1
    result = tap_weights[0] * lax.slice_in_dim(extended, width - 1, width - 1 + out_rows, axis=extended.ndim - 2)
    for position in range(1, width):
        start_row = width - 1 - position
        result = result + tap_weights[position] * lax.slice_in_dim(extended, start_row, start_row + out_rows, axis=extended.ndim - 2)
    return result

def pad_axis(values, amount, axis_back):
    widths = [(0, 0)] * values.ndim
    widths[values.ndim - axis_back] = (amount, amount)
    return jnp.pad(values, widths)

def lev_forward(values, tap_weights):
    radius = tap_weights.shape[0] // 2
    return lat_forward_levels(pad_axis(values, radius, 3), tap_weights, False)

def lev_adjoint(values, tap_weights):
    radius = tap_weights.shape[0] // 2
    return lat_forward_levels(pad_axis(values, radius, 3), tap_weights, True)

def lat_forward_levels(padded, tap_weights, flipped):
    width = tap_weights.shape[0]
    levels = padded.shape[-3] - width + 1
    result = jnp.zeros(padded.shape[:-3] + (levels,) + padded.shape[-2:], padded.dtype)
    for position in range(width):
        start_level = width - 1 - position if flipped else position
        result = result + tap_weights[position] * lax.slice_in_dim(padded, start_level, start_level + levels, axis=padded.ndim - 3)
    return result

def reference(gradient, perturbations, weights, lon_taps, lat_taps, lev_taps, level_order):
    radius = lat_taps.shape[0] // 2
    norm_factor = 1.0 / math.sqrt(MEMBERS - 1)
    grad_levels = jnp.zeros_like(gradient).at[:, level_order].set(gradient)

    def member_step(running, member_item):
        member_pert, member_weights = member_item
        member_pert = member_pert.astype(jnp.float32)
        products = norm_factor * (member_pert[0] * grad_levels[0] + member_pert[1] * grad_levels[1])
        adjoint = lev_adjoint(lon_adjoint(lat_adjoint(pad_axis(products, radius, 2), lat_taps), lon_taps), lev_taps)
        grad_total = member_weights + adjoint
        updated = member_weights - STEP_RATE * grad_total / (1.0 + jnp.abs(grad_total))
        grid_field = lev_forward(lon_forward(lat_forward(pad_axis(updated, radius, 2), lat_taps), lon_taps), lev_taps)
        return (running + norm_factor * member_pert * grid_field[None], updated)
    inc_levels, updated_weights = lax.scan(member_step, jnp.zeros(gradient.shape, jnp.float32), (perturbations, weights))
    return (updated_weights, inc_levels[:, level_order])
```

```python
import functools
import math

import jax
import jax.numpy as jnp
from jax import lax
from jax.experimental import pallas as pl
from jax.experimental.pallas import tpu as pltpu
from jax.sharding import PartitionSpec as P

STEP_RATE = 0.5
TILE = 8
PACK = 16
F32 = jnp.float32
BF16 = jnp.bfloat16


def partner(me, d, n):
    if n & (n - 1):
        return (me + d) % n
    result = 0
    bit = 1
    while bit < n:
        result = result + ((me // bit + d // bit) % 2) * bit
        bit *= 2
    return result


def split(x):
    high = x.astype(BF16)
    return high, (x - high.astype(F32)).astype(BF16)


def dot(a, b):
    return lax.dot_general(a, b, (((1,), (0,)), ((), ())), preferred_element_type=F32)


def filter_lon(x, c_hi, c_lo):
    high, low = split(x)
    return dot(high, c_hi[...]) + (dot(low, c_hi[...]) + dot(high, c_lo[...]))


def stacked(x):
    high, low = split(x)
    return jnp.concatenate([high, high, low], axis=0)


def iota(shape, axis):
    return lax.broadcasted_iota(jnp.int32, shape, axis)


def sizes(rows, radius):
    full = radius // TILE * TILE
    rem = radius - full
    if 2 * rem > TILE or 2 * radius > rows:
        raise NotImplementedError("radius")
    halo = 2 * full + (TILE if rem else 0)
    edge = full + (TILE if rem else 0)
    deep = -(-3 * rows // PACK) * PACK
    wide = -(-(rows + halo) // PACK) * PACK
    return full, rem, halo, edge, deep, wide


def kernel(
    n, bands, norm, radius, lev_width,
    g_hbm, p_hbm, w_hbm, lon_hbm, lat_hbm, lev_hbm, order_hbm,
    u_ref, out_ref,
    g_all, p_ref, pf_ref, w_ref, wn_ref, wh_ref, z_ref, zn_ref, acc_ref, f_ref, inc_ref, rs_ref,
    a_hi, a_lo, b_hi, b_lo, k1, k2,
    lon_t, lat_t, lev_t, order,
    load_sem, known_sem, gs, gr, zs, zr, ws, wr, rss, rsr,
):
    me = lax.axis_index("mem")
    band = lax.axis_index("lat")
    members, _, levels, rows, lons = p_ref.shape
    own_levels = g_hbm.shape[1]
    width = 2 * radius + 1
    full, rem, halo, edge, deep, wide = sizes(rows, radius)
    stack = members * rows
    has_low, has_high = band > 0, band < bands - 1
    mesh_ids = pl.DeviceIdType.MESH

    loads = [
        pltpu.make_async_copy(src, dst, load_sem.at[i])
        for i, (src, dst) in enumerate([
            (g_hbm, g_all.at[0]), (lon_hbm, lon_t), (lat_hbm, lat_t), (lev_hbm, lev_t),
            (order_hbm, order), (p_hbm, p_ref), (w_hbm, w_ref),
        ])
    ]
    load_g, load_lon, load_lat, load_lev, load_order, load_p, load_w = loads
    for copy in loads:
        copy.start()

    barrier = pltpu.get_barrier_semaphore()
    cube = not n & (n - 1)
    direct = [d for d in range(1, n) if not cube or not d & (d - 1)]
    rounds = [[d for d in range(1, n) if not cube or bin(d).count("1") == hops]
              for hops in range(1, len(direct) + 1 if cube else 2)]
    arrival = [0] + [d for ds in rounds for d in ds]

    def greet(semaphore):
        for d in direct:
            pl.semaphore_signal(
                semaphore, inc=1, device_id=(partner(me, d, n), band), device_id_type=mesh_ids
            )

    greet(barrier)

    @pl.when(has_low)
    def _():
        pl.semaphore_signal(barrier, inc=1, device_id=(me, band - 1), device_id_type=mesh_ids)

    @pl.when(has_high)
    def _():
        pl.semaphore_signal(barrier, inc=1, device_id=(me, band + 1), device_id_type=mesh_ids)

    for side, present in ((0, has_low), (1, has_high)):
        @pl.when(jnp.logical_not(present))
        def _():
            for q in range(levels):
                zn_ref[side, q] = jnp.zeros((stack, lons), F32)
            wn_ref[side] = jnp.zeros(wn_ref.shape[1:], F32)

    load_lon.wait()
    row, col = iota((TILE, lons), 0), iota((TILE, lons), 1)
    for c_hi, c_lo, sign in ((a_hi, a_lo, 1), (b_hi, b_lo, -1)):
        off = sign * (col - row) + radius
        off = jnp.where(off < 0, off + lons, off)
        off = jnp.where(off >= lons, off - lons, off)
        base = jnp.zeros((TILE, lons), F32)
        for j in range(width):
            base = jnp.where(off == j, lon_t[j], base)
        for i in range(0, lons, PACK):
            value = jnp.concatenate(
                [pltpu.roll(base, i, 1) if i else base, pltpu.roll(base, i + TILE, 1)], axis=0
            )
            c_hi[i:i + PACK], c_lo[i:i + PACK] = split(value)

    load_lat.wait()

    def thirds(c, size):
        third = (c >= size).astype(jnp.int32) + (c >= 2 * size).astype(jnp.int32)
        return third, c - third * size

    def halo_pos(h):
        s = h - 2 * full
        rest = jnp.where(s < rem, rows + full + s, s - full - TILE)
        rest = jnp.where((s >= rem) & (s < TILE - rem), -4 * rows, rest)
        return jnp.where(h < full, h - full, jnp.where(h < 2 * full, rows + h - full, rest))

    def lat_matrix(out_pos, in_pos, third, sign):
        shift = sign * (in_pos - out_pos)
        value = jnp.zeros(shift.shape, F32)
        for j in range(width):
            value = jnp.where(shift == j - radius, lat_t[j], value)
        high = value.astype(BF16).astype(F32)
        return jnp.where(third == 1, value - high, high).astype(BF16)

    r = iota(k1.shape, 0)
    third, c = thirds(iota(k1.shape, 1), deep)
    out_pos = jnp.where(r < rows, r, halo_pos(r - rows))
    in_pos = jnp.where(c < rows, c, jnp.where(c < 2 * rows, c - 2 * rows, c - rows))
    in_pos = jnp.where(c < 3 * rows, in_pos, 8 * rows)
    k1[...] = lat_matrix(out_pos, in_pos, third, -1)
    r = iota(k2.shape, 0)
    third, c = thirds(iota(k2.shape, 1), wide)
    in_pos = jnp.where(c < rows, c, halo_pos(c - rows))
    in_pos = jnp.where(c < rows + halo, in_pos, 8 * rows)
    inside = (in_pos + band * rows >= 0) & (in_pos + band * rows < bands * rows)
    k2[...] = lat_matrix(r, jnp.where(inside, in_pos, 8 * rows), third, 1)

    def source(d):
        return partner(me, d, n) if cube else (me + n - d) % n

    load_lev.wait()
    load_order.wait()
    level_of = [
        order[source(q // own_levels) * own_levels + q % own_levels] for q in range(levels)
    ]
    coef = []
    for l in range(levels):
        coef.append([])
        for q in range(levels):
            tap = l - level_of[q] + lev_width // 2
            inside = (tap >= 0) & (tap < lev_width)
            value = lev_t[jnp.clip(tap, 0, lev_width - 1)]
            coef[l].append(jnp.where(inside, value, 0.0))

    load_p.wait()
    for q in range(levels):
        for v in range(2):
            for k in range(members):
                pf_ref[q, v, k * rows:(k + 1) * rows] = p_ref[k, v, level_of[q]].astype(F32) * norm
    load_w.wait()
    load_g.wait()

    gathers = {
        d: pltpu.make_async_remote_copy(
            src_ref=g_all.at[0],
            dst_ref=g_all.at[d],
            send_sem=gs.at[d - 1],
            recv_sem=gr.at[d - 1],
            device_id=(partner(me, d, n), band),
            device_id_type=mesh_ids,
        )
        for d in range(1, n)
    }

    def to_bands(low_src, high_src, dst, send_sem, recv_sem):
        def make(side, src, target):
            return pltpu.make_async_remote_copy(
                src_ref=src,
                dst_ref=dst(side),
                send_sem=send_sem(side),
                recv_sem=recv_sem(side),
                device_id=(me, target),
                device_id_type=mesh_ids,
            )

        return make(0, low_src, band + 1), make(1, high_src, band - 1)

    def start(copies):
        pl.when(has_high)(copies[0].start)
        pl.when(has_low)(copies[1].start)

    def wait_recv(copies):
        pl.when(has_low)(copies[0].wait_recv)
        pl.when(has_high)(copies[1].wait_recv)

    def wait_send(copies):
        pl.when(has_high)(copies[0].wait_send)
        pl.when(has_low)(copies[1].wait_send)

    w_copies = to_bands(
        w_ref.at[:, :, rows - edge:rows, :], w_ref.at[:, :, 0:edge, :],
        lambda s: wn_ref.at[s], lambda s: ws.at[s], lambda s: wr.at[s],
    )
    z_copies = [
        to_bands(
            z_ref.at[q], z_ref.at[q],
            lambda s, q=q: zn_ref.at[s, q], lambda s, q=q: zs.at[s, q], lambda s, q=q: zr.at[s, q],
        )
        for q in range(levels)
    ]

    neighbours = has_low.astype(jnp.int32) + has_high.astype(jnp.int32)
    pl.semaphore_wait(barrier, len(direct) + neighbours)
    if len(rounds) > 1:
        greet(known_sem.at[0])
    for d in rounds[0]:
        gathers[d].start()
    start(w_copies)

    def send_level(q):
        d, j = divmod(q, own_levels)
        g0 = jnp.concatenate([g_all[d, 0, j]] * members, axis=0)
        g1 = jnp.concatenate([g_all[d, 1, j]] * members, axis=0)
        z_ref[q] = filter_lon(pf_ref[q, 0] * g0 + pf_ref[q, 1] * g1, a_hi, a_lo)
        start(z_copies[q])

    for j in range(own_levels):
        send_level(j)
    for i in range(1, len(rounds)):
        pl.semaphore_wait(known_sem.at[i - 1], len(direct))
        if i + 1 < len(rounds):
            greet(known_sem.at[i])
        for d in rounds[i]:
            gathers[d].start()
    for d in arrival[1:]:
        gathers[d].wait_recv()
        for j in range(own_levels):
            send_level(d * own_levels + j)

    wait_recv(w_copies)
    s = iota((TILE, lons), 0)
    for k in range(members):
        for l in range(levels):
            wh_ref[k, l, 0:full] = wn_ref[0, k, l, edge - full:edge]
            wh_ref[k, l, full:2 * full] = wn_ref[1, k, l, 0:full]
            if rem:
                wh_ref[k, l, 2 * full:halo] = jnp.where(
                    s < rem, wn_ref[1, k, l, full:edge], wn_ref[0, k, l, 0:TILE]
                )

    ordered = [d * own_levels + j for d in arrival for j in range(own_levels)]
    gap = jnp.zeros((deep - 3 * rows, lons), F32)
    for step, q in enumerate(ordered):
        wait_recv(z_copies[q])
        for k in range(members):
            at = slice(k * rows, (k + 1) * rows)
            x = jnp.concatenate([z_ref[q, at], zn_ref[0, q, at], zn_ref[1, q, at], gap], axis=0)
            y = dot(k1[...], stacked(x))
            if step < levels - 1:
                for l in range(levels):
                    if step:
                        acc_ref[k, l] = acc_ref[k, l] + coef[l][q] * y
                    else:
                        w = jnp.concatenate([w_ref[k, l], wh_ref[k, l]], axis=0)
                        acc_ref[k, l] = w + coef[l][q] * y
                continue
            parts = []
            for l in range(levels):
                w = jnp.concatenate([w_ref[k, l], wh_ref[k, l]], axis=0)
                total = acc_ref[k, l] + coef[l][q] * y
                u = w - STEP_RATE * total / (1.0 + jnp.abs(total))
                u_ref[k, l] = u[0:rows]
                if wide > rows + halo:
                    u = jnp.concatenate([u, jnp.zeros((wide - rows - halo, lons), F32)], axis=0)
                parts.append(dot(k2[...], stacked(u)))
            f_ref[k] = filter_lon(jnp.concatenate(parts, axis=0), b_hi, b_lo)

    scatters = []
    for d in reversed(arrival):
        for j in range(own_levels):
            q = d * own_levels + j
            inc = [jnp.zeros((rows, lons), F32)] * 2
            for k in range(members):
                field = coef[0][q] * f_ref[k, 0:rows]
                for l in range(1, levels):
                    field = field + coef[l][q] * f_ref[k, l * rows:(l + 1) * rows]
                for v in range(2):
                    inc[v] = inc[v] + pf_ref[q, v, k * rows:(k + 1) * rows] * field
            for v in range(2):
                inc_ref[d, v, j] = inc[v]
        if d:
            scatters.append(
                pltpu.make_async_remote_copy(
                    src_ref=inc_ref.at[d],
                    dst_ref=rs_ref.at[d - 1],
                    send_sem=rss.at[d - 1],
                    recv_sem=rsr.at[d - 1],
                    device_id=(source(d), band),
                    device_id_type=mesh_ids,
                )
            )
            scatters[-1].start()
    wait_send(w_copies)
    for copies in z_copies:
        wait_send(copies)
    for copy in gathers.values():
        copy.wait_send()
    result = inc_ref[0]
    for copy, d in zip(scatters, [d for d in reversed(arrival) if d]):
        copy.wait_recv()
        result = result + rs_ref[d - 1]
    out_ref[...] = result
    for copy in scatters:
        copy.wait_send()


def write_out(u_ref, inc_ref, upd_hbm, inc_hbm, sem):
    first = pltpu.make_async_copy(u_ref, upd_hbm, sem.at[0])
    second = pltpu.make_async_copy(inc_ref, inc_hbm, sem.at[1])
    first.start()
    second.start()
    first.wait()
    second.wait()


def on_device(gradient, perturbations, weights, lon_taps, lat_taps, lev_taps, level_order):
    n, bands = lax.axis_size("mem"), lax.axis_size("lat")
    members, levels, rows, lons = weights.shape
    radius = lat_taps.shape[0] // 2
    norm = 1.0 / math.sqrt(members * n - 1)
    full, rem, halo, edge, deep, wide = sizes(rows, radius)
    stack = members * rows
    vmem, dma = pltpu.VMEM, pltpu.SemaphoreType.DMA
    anywhere = pl.BlockSpec(memory_space=pl.ANY)
    in_vmem = pl.BlockSpec(memory_space=pltpu.VMEM)
    updated, increment = pl.pallas_call(
        functools.partial(kernel, n, bands, norm, radius, lev_taps.shape[0]),
        out_shape=(
            vmem(weights.shape, F32),
            vmem(gradient.shape, F32),
        ),
        in_specs=[anywhere] * 7,
        out_specs=(in_vmem, in_vmem),
        scratch_shapes=[
            vmem((n,) + gradient.shape, F32),
            vmem(perturbations.shape, BF16),
            vmem((levels, 2, stack, lons), F32),
            vmem(weights.shape, F32),
            vmem((2, members, levels, edge, lons), F32),
            vmem((members, levels, halo, lons), F32),
            vmem((levels, stack, lons), F32),
            vmem((2, levels, stack, lons), F32),
            vmem((members, levels, rows + halo, lons), F32),
            vmem((members, levels * rows, lons), F32),
            vmem((n,) + gradient.shape, F32),
            vmem((n - 1,) + gradient.shape, F32),
            vmem((lons, lons), BF16),
            vmem((lons, lons), BF16),
            vmem((lons, lons), BF16),
            vmem((lons, lons), BF16),
            vmem((rows + halo, 3 * deep), BF16),
            vmem((rows, 3 * wide), BF16),
            pltpu.SMEM(lon_taps.shape, F32),
            pltpu.SMEM(lat_taps.shape, F32),
            pltpu.SMEM(lev_taps.shape, F32),
            pltpu.SMEM(level_order.shape, jnp.int32),
            dma((7,)),
            pltpu.SemaphoreType.REGULAR((max(1, n.bit_length() - 2),)),
            dma((n - 1,)),
            dma((n - 1,)),
            dma((2, levels)),
            dma((2, levels)),
            dma((2,)),
            dma((2,)),
            dma((n - 1,)),
            dma((n - 1,)),
        ],
        compiler_params=pltpu.CompilerParams(collective_id=0, has_side_effects=True),
        name="step",
    )(gradient, perturbations, weights, lon_taps, lat_taps, lev_taps, level_order)
    return pl.pallas_call(
        write_out,
        out_shape=(
            jax.ShapeDtypeStruct(updated.shape, F32),
            jax.ShapeDtypeStruct(increment.shape, F32),
        ),
        in_specs=[in_vmem] * 2,
        out_specs=(anywhere, anywhere),
        scratch_shapes=[dma((2,))],
        name="write_out",
    )(
        pltpu.with_memory_space_constraint(updated, pltpu.VMEM),
        pltpu.with_memory_space_constraint(increment, pltpu.VMEM),
    )


def solution(mesh):
    in_specs = (
        P(None, "mem", "lat", None),
        P("mem", None, None, "lat", None),
        P("mem", None, "lat", None),
        P(),
        P(),
        P(),
        P(),
    )
    out_specs = (P("mem", None, "lat", None), P(None, "mem", "lat", None))
    return jax.shard_map(
        on_device, mesh=mesh, in_specs=in_specs, out_specs=out_specs, check_vma=False
    )
```

```python
import functools
import math

import jax
import jax.numpy as jnp
from jax import lax
from jax.experimental import pallas as pl
from jax.experimental.pallas import tpu as pltpu
from jax.sharding import PartitionSpec as P

STEP_RATE = 0.5
TILE = 8
PACK = 16
F32 = jnp.float32
BF16 = jnp.bfloat16


def partner(me, d, n):
    if n & (n - 1):
        return (me + d) % n
    result = 0
    bit = 1
    while bit < n:
        result = result + ((me // bit + d // bit) % 2) * bit
        bit *= 2
    return result


def split(x):
    high = x.astype(BF16)
    return high, (x - high.astype(F32)).astype(BF16)


def dot(a, b):
    return lax.dot_general(a, b, (((1,), (0,)), ((), ())), preferred_element_type=F32)


def filter_lon(x, c_hi, c_lo):
    high, low = split(x)
    both = dot(jnp.concatenate([high, low], axis=0), c_hi[...])
    return both[:x.shape[0]] + (both[x.shape[0]:] + dot(high, c_lo[...]))


def packed(rows):
    return -(-rows // PACK) * PACK


def stacked(x):
    pad = packed(x.shape[0]) - x.shape[0]
    if pad:
        x = jnp.concatenate([x, jnp.zeros((pad, x.shape[1]), F32)], axis=0)
    high, low = split(x)
    return jnp.concatenate([high, high, low], axis=0)


def iota(shape, axis):
    return lax.broadcasted_iota(jnp.int32, shape, axis)


def sizes(rows, radius):
    full = radius // TILE * TILE
    rem = radius - full
    if 2 * rem > TILE or 2 * radius > rows:
        raise NotImplementedError("radius")
    halo = 2 * full + (TILE if rem else 0)
    edge = full + (TILE if rem else 0)
    return full, rem, halo, edge


def kernel(
    n, bands, norm, radius, lev_width,
    g_hbm, p_hbm, w_hbm, lon_hbm, lat_hbm, lev_hbm, order_hbm,
    u_ref, out_ref,
    g_all, p_ref, pf_ref, w_ref, wn_ref, wh_ref, z_ref, zn_ref, acc_ref, f_ref, inc_ref, rs_ref,
    a_hi, a_lo, b_hi, b_lo, k_own, k_halo, k_fwd,
    lon_t, lat_t, lev_t, order,
    load_sem, known_sem, gs, gr, zs, zr, ws, wr, rsr,
):
    me = lax.axis_index("mem")
    band = lax.axis_index("lat")
    members, _, levels, rows, lons = p_ref.shape
    own_levels = g_hbm.shape[1]
    width = 2 * radius + 1
    full, rem, halo, edge = sizes(rows, radius)
    stack = members * rows
    has_low, has_high = band > 0, band < bands - 1
    mesh_ids = pl.DeviceIdType.MESH

    loads = [
        pltpu.make_async_copy(src, dst, load_sem.at[i])
        for i, (src, dst) in enumerate([
            (g_hbm, g_all.at[0]), (w_hbm, w_ref), (lon_hbm, lon_t), (order_hbm, order),
            (p_hbm, p_ref), (lev_hbm, lev_t), (lat_hbm, lat_t),
        ])
    ]
    load_g, load_w, load_lon, load_order, load_p, load_lev, load_lat = loads
    for copy in loads:
        copy.start()

    barrier = pltpu.get_barrier_semaphore()
    cube = not n & (n - 1)
    direct = [d for d in range(1, n) if not cube or not d & (d - 1)]
    rounds = [[d for d in range(1, n) if not cube or bin(d).count("1") == hops]
              for hops in range(1, len(direct) + 1 if cube else 2)]
    arrival = [0] + [d for ds in rounds for d in ds]

    def greet(semaphore):
        for d in direct:
            pl.semaphore_signal(
                semaphore, inc=1, device_id=(partner(me, d, n), band), device_id_type=mesh_ids
            )

    greet(barrier)

    @pl.when(has_low)
    def _():
        pl.semaphore_signal(barrier, inc=1, device_id=(me, band - 1), device_id_type=mesh_ids)

    @pl.when(has_high)
    def _():
        pl.semaphore_signal(barrier, inc=1, device_id=(me, band + 1), device_id_type=mesh_ids)

    def source(d):
        return partner(me, d, n) if cube else (me + n - d) % n

    gathers = {
        d: pltpu.make_async_remote_copy(
            src_ref=g_all.at[0],
            dst_ref=g_all.at[d],
            send_sem=gs.at[d - 1],
            recv_sem=gr.at[d - 1],
            device_id=(partner(me, d, n), band),
            device_id_type=mesh_ids,
        )
        for d in range(1, n)
    }

    def to_bands(low_src, high_src, dst, send_sem, recv_sem):
        def make(side, src, target):
            return pltpu.make_async_remote_copy(
                src_ref=src,
                dst_ref=dst(side),
                send_sem=send_sem(side),
                recv_sem=recv_sem(side),
                device_id=(me, target),
                device_id_type=mesh_ids,
            )

        return make(0, low_src, band + 1), make(1, high_src, band - 1)

    def start(copies):
        pl.when(has_high)(copies[0].start)
        pl.when(has_low)(copies[1].start)

    def wait_recv(copies):
        pl.when(has_low)(copies[0].wait_recv)
        pl.when(has_high)(copies[1].wait_recv)

    def wait_send(copies):
        pl.when(has_high)(copies[0].wait_send)
        pl.when(has_low)(copies[1].wait_send)

    def w_copy(i, size, low, high):
        at = low - rows + edge, high
        return to_bands(
            w_ref.at[:, :, low:low + size, :], w_ref.at[:, :, high:high + size, :],
            lambda s: wn_ref.at[s, :, :, at[s]:at[s] + size, :],
            lambda s: ws.at[s, i], lambda s: wr.at[s, i],
        )

    w_copies = [w_copy(0, full, rows - full, 0)]
    if rem:
        w_copies.append(w_copy(1, rem, rows - radius, full))
    z_copies = [
        to_bands(
            z_ref.at[q], z_ref.at[q],
            lambda s, q=q: zn_ref.at[s, q], lambda s, q=q: zs.at[s, q], lambda s, q=q: zr.at[s, q],
        )
        for q in range(levels)
    ]

    load_g.wait()
    neighbours = has_low.astype(jnp.int32) + has_high.astype(jnp.int32)
    pl.semaphore_wait(barrier, len(direct) + neighbours)
    if len(rounds) > 1:
        greet(known_sem.at[0])
    for d in rounds[0]:
        gathers[d].start()
    load_w.wait()
    for copies in w_copies:
        start(copies)

    row, col = iota((TILE, lons), 0), iota((TILE, lons), 1)

    def lon_matrix(c_hi, c_lo, sign):
        off = sign * (col - row) + radius
        off = jnp.where(off < 0, off + lons, off)
        off = jnp.where(off >= lons, off - lons, off)
        base = jnp.zeros((TILE, lons), F32)
        for j in range(width):
            base = jnp.where(off == j, lon_t[j], base)
        for i in range(0, lons, PACK):
            value = jnp.concatenate(
                [pltpu.roll(base, i, 1) if i else base, pltpu.roll(base, i + TILE, 1)], axis=0
            )
            c_hi[i:i + PACK], c_lo[i:i + PACK] = split(value)

    load_lon.wait()
    lon_matrix(a_hi, a_lo, 1)
    load_order.wait()
    level_of = [
        order[source(q // own_levels) * own_levels + q % own_levels] for q in range(levels)
    ]
    load_p.wait()

    def scaled(q):
        for v in range(2):
            for k in range(members):
                pf_ref[q, v, k * rows:(k + 1) * rows] = p_ref[k, v, level_of[q]].astype(F32) * norm

    def send_level(q):
        d, j = divmod(q, own_levels)
        g0 = jnp.concatenate([g_all[d, 0, j]] * members, axis=0)
        g1 = jnp.concatenate([g_all[d, 1, j]] * members, axis=0)
        z_ref[q] = filter_lon(pf_ref[q, 0] * g0 + pf_ref[q, 1] * g1, a_hi, a_lo)
        start(z_copies[q])

    for j in range(own_levels):
        scaled(j)
        send_level(j)
    for i in range(1, len(rounds)):
        pl.semaphore_wait(known_sem.at[i - 1], len(direct))
        if i + 1 < len(rounds):
            greet(known_sem.at[i])
        for d in rounds[i]:
            gathers[d].start()

    for q in range(own_levels, levels):
        scaled(q)
    for side, present in ((0, has_low), (1, has_high)):
        @pl.when(jnp.logical_not(present))
        def _():
            for q in range(levels):
                zn_ref[side, q] = jnp.zeros((stack, lons), F32)
            wn_ref[side] = jnp.zeros(wn_ref.shape[1:], F32)

    lon_matrix(b_hi, b_lo, -1)
    load_lat.wait()

    def thirds(shape):
        c, size = iota(shape, 1), shape[1] // 3
        third = (c >= size).astype(jnp.int32) + (c >= 2 * size).astype(jnp.int32)
        return third, c - third * size

    def halo_pos(h):
        s = h - 2 * full
        rest = jnp.where(s < rem, rows + full + s, s - full - TILE)
        rest = jnp.where((s >= rem) & (s < TILE - rem), -4 * rows, rest)
        return jnp.where(h < full, h - full, jnp.where(h < 2 * full, rows + h - full, rest))

    def lat_matrix(out_pos, in_pos, third, sign):
        shift = sign * (in_pos - out_pos)
        value = jnp.zeros(shift.shape, F32)
        for j in range(width):
            value = jnp.where(shift == j - radius, lat_t[j], value)
        high = value.astype(BF16).astype(F32)
        return jnp.where(third == 1, value - high, high).astype(BF16)

    far = 8 * rows
    for k_ref, is_own in ((k_own, True), (k_halo, False)):
        r = iota(k_ref.shape, 0)
        third, c = thirds(k_ref.shape)
        if is_own:
            in_pos = jnp.where(c < rows, c, far)
        else:
            in_pos = jnp.where(c < rows, c - rows, jnp.where(c < 2 * rows, c, far))
        out_pos = jnp.where(r < rows, r, halo_pos(r - rows))
        k_ref[...] = lat_matrix(out_pos, in_pos, third, -1)
    third, c = thirds(k_fwd.shape)
    in_pos = jnp.where(c < rows, c, halo_pos(c - rows))
    inside = (in_pos + band * rows >= 0) & (in_pos + band * rows < bands * rows)
    inside = inside & (c < rows + halo)
    k_fwd[...] = lat_matrix(iota(k_fwd.shape, 0), jnp.where(inside, in_pos, far), third, 1)

    load_lev.wait()
    coef = []
    for l in range(levels):
        coef.append([])
        for q in range(levels):
            tap = l - level_of[q] + lev_width // 2
            inside = (tap >= 0) & (tap < lev_width)
            value = lev_t[jnp.clip(tap, 0, lev_width - 1)]
            coef[l].append(jnp.where(inside, value, 0.0))

    for d in arrival[1:]:
        gathers[d].wait_recv()
        for j in range(own_levels):
            send_level(d * own_levels + j)

    for copies in w_copies:
        wait_recv(copies)
    s = iota((TILE, lons), 0)
    for k in range(members):
        at = slice(k * rows, (k + 1) * rows)
        for l in range(levels):
            wh_ref[k, l, 0:full] = wn_ref[0, k, l, edge - full:edge]
            wh_ref[k, l, full:2 * full] = wn_ref[1, k, l, 0:full]
            if rem:
                wh_ref[k, l, 2 * full:halo] = jnp.where(
                    s < rem, wn_ref[1, k, l, full:edge], wn_ref[0, k, l, 0:TILE]
                )
        own = [dot(k_own[...], stacked(z_ref[q, at])) for q in range(levels)]
        for l in range(levels):
            total = jnp.concatenate([w_ref[k, l], wh_ref[k, l]], axis=0)
            for q in range(levels):
                total = total + coef[l][q] * own[q]
            acc_ref[k, l] = total
    for copies in w_copies:
        wait_send(copies)
    for copy in gathers.values():
        copy.wait_send()

    ordered = [d * own_levels + j for d in arrival for j in range(own_levels)]
    for q in ordered[:-1]:
        wait_recv(z_copies[q])
        for k in range(members):
            at = slice(k * rows, (k + 1) * rows)
            y = dot(k_halo[...], stacked(jnp.concatenate([zn_ref[0, q, at], zn_ref[1, q, at]], axis=0)))
            for l in range(levels):
                acc_ref[k, l] = acc_ref[k, l] + coef[l][q] * y
        wait_send(z_copies[q])

    q = ordered[-1]
    wait_recv(z_copies[q])
    for k in range(members):
        at = slice(k * rows, (k + 1) * rows)
        y = dot(k_halo[...], stacked(jnp.concatenate([zn_ref[0, q, at], zn_ref[1, q, at]], axis=0)))
        for l in range(levels):
            w = jnp.concatenate([w_ref[k, l], wh_ref[k, l]], axis=0)
            total = acc_ref[k, l] + coef[l][q] * y
            u = w - STEP_RATE * total / (1.0 + jnp.abs(total))
            u_ref[k, l] = u[0:rows]
            f_ref[k, l] = dot(k_fwd[...], stacked(u))

    fields = []
    for d in reversed(arrival):
        for j in range(own_levels):
            for k in range(members):
                field = coef[0][d * own_levels + j] * f_ref[k, 0]
                for l in range(1, levels):
                    field = field + coef[l][d * own_levels + j] * f_ref[k, l]
                fields.append(field)
    fields = filter_lon(jnp.concatenate(fields, axis=0), b_hi, b_lo)

    scatters = []
    for i, d in enumerate(reversed(arrival)):
        for j in range(own_levels):
            q = d * own_levels + j
            at = (i * own_levels + j) * stack
            for v in range(2):
                terms = pf_ref[q, v] * fields[at:at + stack]
                inc = terms[0:rows]
                for k in range(1, members):
                    inc = inc + terms[k * rows:(k + 1) * rows]
                inc_ref[d, v, j] = inc
        if d:
            scatters.append(
                pltpu.make_async_remote_copy(
                    src_ref=inc_ref.at[d],
                    dst_ref=rs_ref.at[d - 1],
                    send_sem=gs.at[d - 1],
                    recv_sem=rsr.at[d - 1],
                    device_id=(source(d), band),
                    device_id_type=mesh_ids,
                )
            )
            scatters[-1].start()
    wait_send(z_copies[ordered[-1]])
    result = inc_ref[0]
    for copy, d in zip(scatters, [d for d in reversed(arrival) if d]):
        copy.wait_recv()
        result = result + rs_ref[d - 1]
    out_ref[...] = result
    for copy in scatters:
        copy.wait_send()


def write_out(u_ref, inc_ref, upd_hbm, inc_hbm, sem):
    first = pltpu.make_async_copy(u_ref, upd_hbm, sem.at[0])
    second = pltpu.make_async_copy(inc_ref, inc_hbm, sem.at[1])
    first.start()
    second.start()
    first.wait()
    second.wait()


def on_device(gradient, perturbations, weights, lon_taps, lat_taps, lev_taps, level_order):
    n, bands = lax.axis_size("mem"), lax.axis_size("lat")
    members, levels, rows, lons = weights.shape
    radius = lat_taps.shape[0] // 2
    norm = 1.0 / math.sqrt(members * n - 1)
    full, rem, halo, edge = sizes(rows, radius)
    stack = members * rows
    vmem, dma = pltpu.VMEM, pltpu.SemaphoreType.DMA
    anywhere = pl.BlockSpec(memory_space=pl.ANY)
    in_vmem = pl.BlockSpec(memory_space=pltpu.VMEM)
    updated, increment = pl.pallas_call(
        functools.partial(kernel, n, bands, norm, radius, lev_taps.shape[0]),
        out_shape=(
            vmem(weights.shape, F32),
            vmem(gradient.shape, F32),
        ),
        in_specs=[anywhere] * 7,
        out_specs=(in_vmem, in_vmem),
        scratch_shapes=[
            vmem((n,) + gradient.shape, F32),
            vmem(perturbations.shape, BF16),
            vmem((levels, 2, stack, lons), F32),
            vmem(weights.shape, F32),
            vmem((2, members, levels, edge, lons), F32),
            vmem((members, levels, halo, lons), F32),
            vmem((levels, stack, lons), F32),
            vmem((2, levels, stack, lons), F32),
            vmem((members, levels, rows + halo, lons), F32),
            vmem(weights.shape, F32),
            vmem((n,) + gradient.shape, F32),
            vmem((n - 1,) + gradient.shape, F32),
            vmem((lons, lons), BF16),
            vmem((lons, lons), BF16),
            vmem((lons, lons), BF16),
            vmem((lons, lons), BF16),
            vmem((rows + halo, 3 * packed(rows)), BF16),
            vmem((rows + halo, 3 * packed(2 * rows)), BF16),
            vmem((rows, 3 * packed(rows + halo)), BF16),
            pltpu.SMEM(lon_taps.shape, F32),
            pltpu.SMEM(lat_taps.shape, F32),
            pltpu.SMEM(lev_taps.shape, F32),
            pltpu.SMEM(level_order.shape, jnp.int32),
            dma((7,)),
            pltpu.SemaphoreType.REGULAR((max(1, n.bit_length() - 2),)),
            dma((n - 1,)),
            dma((n - 1,)),
            dma((2, levels)),
            dma((2, levels)),
            dma((2, 2)),
            dma((2, 2)),
            dma((n - 1,)),
        ],
        compiler_params=pltpu.CompilerParams(collective_id=0, has_side_effects=True),
        name="step",
    )(gradient, perturbations, weights, lon_taps, lat_taps, lev_taps, level_order)
    return pl.pallas_call(
        write_out,
        out_shape=(
            jax.ShapeDtypeStruct(updated.shape, F32),
            jax.ShapeDtypeStruct(increment.shape, F32),
        ),
        in_specs=[in_vmem] * 2,
        out_specs=(anywhere, anywhere),
        scratch_shapes=[dma((2,))],
        name="write_out",
    )(
        pltpu.with_memory_space_constraint(updated, pltpu.VMEM),
        pltpu.with_memory_space_constraint(increment, pltpu.VMEM),
    )


def solution(mesh):
    in_specs = (
        P(None, "mem", "lat", None),
        P("mem", None, None, "lat", None),
        P("mem", None, "lat", None),
        P(),
        P(),
        P(),
        P(),
    )
    out_specs = (P("mem", None, "lat", None), P(None, "mem", "lat", None))
    return jax.shard_map(
        on_device, mesh=mesh, in_specs=in_specs, out_specs=out_specs, check_vma=False
    )
```

```python
import functools
import math

import jax
import jax.numpy as jnp
from jax import lax
from jax.experimental import pallas as pl
from jax.experimental.pallas import tpu as pltpu
from jax.sharding import PartitionSpec as P

STEP_RATE = 0.5
TILE = 8
PACK = 16
F32 = jnp.float32
BF16 = jnp.bfloat16


def partner(me, d, n):
    if n & (n - 1):
        return (me + d) % n
    result = 0
    bit = 1
    while bit < n:
        result = result + ((me // bit + d // bit) % 2) * bit
        bit *= 2
    return result


def split(x):
    high = x.astype(BF16)
    return high, (x - high.astype(F32)).astype(BF16)


def dot(a, b):
    return lax.dot_general(a, b, (((1,), (0,)), ((), ())), preferred_element_type=F32)


def filter_lon(x, c_hi, c_lo):
    high, low = split(x)
    both = dot(jnp.concatenate([high, low], axis=0), c_hi[...])
    return both[:x.shape[0]] + (both[x.shape[0]:] + dot(high, c_lo[...]))


def packed(rows):
    return -(-rows // PACK) * PACK


def stacked(x):
    pad = packed(x.shape[0]) - x.shape[0]
    if pad:
        x = jnp.concatenate([x, jnp.zeros((pad, x.shape[1]), F32)], axis=0)
    high, low = split(x)
    return jnp.concatenate([high, high, low], axis=0)


def iota(shape, axis):
    return lax.broadcasted_iota(jnp.int32, shape, axis)


def sizes(rows, radius):
    full = radius // TILE * TILE
    rem = radius - full
    if 2 * rem > TILE or 2 * radius > rows:
        raise NotImplementedError("radius")
    halo = 2 * full + (TILE if rem else 0)
    edge = full + (TILE if rem else 0)
    return full, rem, halo, edge


def kernel(
    n, bands, norm, radius, lev_width,
    g_hbm, p_hbm, w_hbm, lon_hbm, lat_hbm, lev_hbm, order_hbm,
    u_ref, out_ref,
    g_all, p_ref, pf_ref, w_ref, wn_ref, wh_ref, z_ref, zn_ref, acc_ref, f_ref, inc_ref, rs_ref,
    a_hi, a_lo, b_hi, b_lo, k_own, k_halo, k_fwd,
    lon_t, lat_t, lev_t, order,
    pool, known_sem, gr, zr, wr, rsr,
):
    me = lax.axis_index("mem")
    band = lax.axis_index("lat")
    members, _, levels, rows, lons = p_ref.shape
    own_levels = g_hbm.shape[1]
    width = 2 * radius + 1
    full, rem, halo, edge = sizes(rows, radius)
    stack = members * rows
    has_low, has_high = band > 0, band < bands - 1
    mesh_ids = pl.DeviceIdType.MESH

    free = list(range(pool.shape[0]))
    loads = [
        pltpu.make_async_copy(src, dst, pool.at[free.pop(0)])
        for i, (src, dst) in enumerate([
            (g_hbm, g_all.at[0]), (w_hbm, w_ref), (lon_hbm, lon_t), (order_hbm, order),
            (p_hbm, p_ref), (lev_hbm, lev_t), (lat_hbm, lat_t),
        ])
    ]
    g_in, w_in, lon_in, order_in, p_in, lev_in, lat_in = range(len(loads))
    for copy in loads:
        copy.start()

    barrier = pltpu.get_barrier_semaphore()
    cube = not n & (n - 1)
    direct = [d for d in range(1, n) if not cube or not d & (d - 1)]
    rounds = [[d for d in range(1, n) if not cube or bin(d).count("1") == hops]
              for hops in range(1, len(direct) + 1 if cube else 2)]
    arrival = [0] + [d for ds in rounds for d in ds]

    def greet(semaphore):
        for d in direct:
            pl.semaphore_signal(
                semaphore, inc=1, device_id=(partner(me, d, n), band), device_id_type=mesh_ids
            )

    greet(barrier)

    @pl.when(has_low)
    def _():
        pl.semaphore_signal(barrier, inc=1, device_id=(me, band - 1), device_id_type=mesh_ids)

    @pl.when(has_high)
    def _():
        pl.semaphore_signal(barrier, inc=1, device_id=(me, band + 1), device_id_type=mesh_ids)

    def source(d):
        return partner(me, d, n) if cube else (me + n - d) % n

    sent = []

    def remote(src, dst, recv_sem, sem, target):
        return pltpu.make_async_remote_copy(
            src_ref=src,
            dst_ref=dst,
            send_sem=pool.at[sem],
            recv_sem=recv_sem,
            device_id=target,
            device_id_type=mesh_ids,
        )

    def gather(d):
        sem = free.pop(0)
        copy = remote(g_all.at[0], g_all.at[d], gr.at[d - 1], sem, (partner(me, d, n), band))
        copy.start()
        sent.append((sem, copy.wait_send))
        return copy

    odd = band % 2
    far_then_near = ((1 - odd, band - 1 + 2 * odd), (odd, band + 1 - 2 * odd))
    both = has_low & has_high
    one = has_low ^ has_high

    def to_bands(pairs, piece, whole, recv_sem):
        sem = free.pop(0)
        for side, target in pairs:
            @pl.when((target >= 0) & (target < bands))
            def _():
                remote(*piece(side), recv_sem, sem, (me, target)).start()

        def wait(semaphore):
            for count, here in ((2, both), (1, one)):
                ref = whole(count)
                pl.when(here)(pltpu.make_async_copy(ref, ref, semaphore).wait)

        sent.append((sem, lambda: wait(pool.at[sem])))
        return lambda: wait(recv_sem)

    def send_weights(size, low, high, recv_sem):
        at = ((low, low - rows + edge), (high, high))
        return to_bands(
            ((0, band + 1), (1, band - 1)),
            lambda side: (
                w_ref.at[:, :, at[side][0]:at[side][0] + size, :],
                wn_ref.at[side, :, :, at[side][1]:at[side][1] + size, :],
            ),
            lambda count: wn_ref.at[0:count, :, :, 0:size, :],
            recv_sem,
        )

    def settle(keep=0):
        for sem, wait in sent[:len(sent) - keep]:
            wait()
            free.append(sem)
        del sent[:len(sent) - keep]

    def loaded(i):
        loads[i].wait()
        free.append(i)

    loaded(g_in)
    neighbours = has_low.astype(jnp.int32) + has_high.astype(jnp.int32)
    pl.semaphore_wait(barrier, len(direct) + neighbours)
    if len(rounds) > 1:
        greet(known_sem.at[0])
    gathers = {d: gather(d) for d in rounds[0]}
    loaded(w_in)
    w_arrival = [send_weights(full, rows - full, 0, wr.at[0])]
    if rem:
        w_arrival.append(send_weights(rem, rows - radius, full, wr.at[1]))

    row, col = iota((TILE, lons), 0), iota((TILE, lons), 1)

    def lon_matrix(c_hi, c_lo, sign):
        off = sign * (col - row) + radius
        off = jnp.where(off < 0, off + lons, off)
        off = jnp.where(off >= lons, off - lons, off)
        base = jnp.zeros((TILE, lons), F32)
        for j in range(width):
            base = jnp.where(off == j, lon_t[j], base)
        for i in range(0, lons, PACK):
            value = jnp.concatenate(
                [pltpu.roll(base, i, 1) if i else base, pltpu.roll(base, i + TILE, 1)], axis=0
            )
            c_hi[i:i + PACK], c_lo[i:i + PACK] = split(value)

    loaded(lon_in)
    lon_matrix(a_hi, a_lo, 1)
    loaded(order_in)
    level_of = [
        order[source(q // own_levels) * own_levels + q % own_levels] for q in range(levels)
    ]
    loaded(p_in)

    def scaled(q):
        for v in range(2):
            for k in range(members):
                pf_ref[q, v, k * rows:(k + 1) * rows] = p_ref[k, v, level_of[q]].astype(F32) * norm

    z_arrival = {}

    def send_level(q):
        d, j = divmod(q, own_levels)
        g0 = jnp.concatenate([g_all[d, 0, j]] * members, axis=0)
        g1 = jnp.concatenate([g_all[d, 1, j]] * members, axis=0)
        z_ref[q] = filter_lon(pf_ref[q, 0] * g0 + pf_ref[q, 1] * g1, a_hi, a_lo)
        z_arrival[q] = to_bands(
            far_then_near, lambda side: (z_ref.at[q], zn_ref.at[side, q]),
            lambda count: zn_ref.at[0:count, q], zr.at[q],
        )

    for j in range(own_levels):
        scaled(j)
        send_level(j)
    for i in range(1, len(rounds)):
        pl.semaphore_wait(known_sem.at[i - 1], len(direct))
        if i + 1 < len(rounds):
            greet(known_sem.at[i])
        gathers.update({d: gather(d) for d in rounds[i]})

    for q in range(own_levels, levels):
        scaled(q)
    for side, present in ((0, has_low), (1, has_high)):
        @pl.when(jnp.logical_not(present))
        def _():
            for q in range(levels):
                zn_ref[side, q] = jnp.zeros((stack, lons), F32)
            wn_ref[side] = jnp.zeros(wn_ref.shape[1:], F32)

    lon_matrix(b_hi, b_lo, -1)
    loaded(lat_in)

    def thirds(shape):
        c, size = iota(shape, 1), shape[1] // 3
        third = (c >= size).astype(jnp.int32) + (c >= 2 * size).astype(jnp.int32)
        return third, c - third * size

    def halo_pos(h):
        s = h - 2 * full
        rest = jnp.where(s < rem, rows + full + s, s - full - TILE)
        rest = jnp.where((s >= rem) & (s < TILE - rem), -4 * rows, rest)
        return jnp.where(h < full, h - full, jnp.where(h < 2 * full, rows + h - full, rest))

    def lat_matrix(out_pos, in_pos, third, sign):
        shift = sign * (in_pos - out_pos)
        value = jnp.zeros(shift.shape, F32)
        for j in range(width):
            value = jnp.where(shift == j - radius, lat_t[j], value)
        high = value.astype(BF16).astype(F32)
        return jnp.where(third == 1, value - high, high).astype(BF16)

    far = 8 * rows
    for k_ref, is_own in ((k_own, True), (k_halo, False)):
        r = iota(k_ref.shape, 0)
        third, c = thirds(k_ref.shape)
        if is_own:
            in_pos = jnp.where(c < rows, c, far)
        else:
            in_pos = jnp.where(c < rows, c - rows, jnp.where(c < 2 * rows, c, far))
        out_pos = jnp.where(r < rows, r, halo_pos(r - rows))
        k_ref[...] = lat_matrix(out_pos, in_pos, third, -1)
    third, c = thirds(k_fwd.shape)
    in_pos = jnp.where(c < rows, c, halo_pos(c - rows))
    inside = (in_pos + band * rows >= 0) & (in_pos + band * rows < bands * rows)
    inside = inside & (c < rows + halo)
    k_fwd[...] = lat_matrix(iota(k_fwd.shape, 0), jnp.where(inside, in_pos, far), third, 1)

    loaded(lev_in)
    coef = []
    for l in range(levels):
        coef.append([])
        for q in range(levels):
            tap = l - level_of[q] + lev_width // 2
            inside = (tap >= 0) & (tap < lev_width)
            value = lev_t[jnp.clip(tap, 0, lev_width - 1)]
            coef[l].append(jnp.where(inside, value, 0.0))

    for d in arrival[1:]:
        gathers[d].wait_recv()
        for j in range(own_levels):
            send_level(d * own_levels + j)

    for wait in w_arrival:
        wait()
    s = iota((TILE, lons), 0)
    for k in range(members):
        at = slice(k * rows, (k + 1) * rows)
        for l in range(levels):
            wh_ref[k, l, 0:full] = wn_ref[0, k, l, edge - full:edge]
            wh_ref[k, l, full:2 * full] = wn_ref[1, k, l, 0:full]
            if rem:
                wh_ref[k, l, 2 * full:halo] = jnp.where(
                    s < rem, wn_ref[1, k, l, full:edge], wn_ref[0, k, l, 0:TILE]
                )
        own = [dot(k_own[...], stacked(z_ref[q, at])) for q in range(levels)]
        for l in range(levels):
            total = jnp.concatenate([w_ref[k, l], wh_ref[k, l]], axis=0)
            for q in range(levels):
                total = total + coef[l][q] * own[q]
            acc_ref[k, l] = total

    ordered = [d * own_levels + j for d in arrival for j in range(own_levels)]
    for q in ordered[:-1]:
        z_arrival[q]()
        for k in range(members):
            at = slice(k * rows, (k + 1) * rows)
            y = dot(k_halo[...], stacked(jnp.concatenate([zn_ref[0, q, at], zn_ref[1, q, at]], axis=0)))
            for l in range(levels):
                acc_ref[k, l] = acc_ref[k, l] + coef[l][q] * y

    settle(keep=1)
    q = ordered[-1]
    z_arrival[q]()
    last = []
    for k in range(members):
        at = slice(k * rows, (k + 1) * rows)
        x = jnp.concatenate([zn_ref[0, q, at], zn_ref[1, q, at]], axis=0)
        last.append(dot(k_halo[...], stacked(x)))
    for k in range(members):
        for l in range(levels):
            w = jnp.concatenate([w_ref[k, l], wh_ref[k, l]], axis=0)
            total = acc_ref[k, l] + coef[l][q] * last[k]
            u = w - STEP_RATE * total / (1.0 + jnp.abs(total))
            u_ref[k, l] = u[0:rows]
            f_ref[k, l] = dot(k_fwd[...], stacked(u))

    fields = []
    for d in reversed(arrival):
        for j in range(own_levels):
            for k in range(members):
                field = coef[0][d * own_levels + j] * f_ref[k, 0]
                for l in range(1, levels):
                    field = field + coef[l][d * own_levels + j] * f_ref[k, l]
                fields.append(field)
    fields = filter_lon(jnp.concatenate(fields, axis=0), b_hi, b_lo)

    scatter_sem = free.pop(0)
    for i, d in enumerate(reversed(arrival)):
        for j in range(own_levels):
            q = d * own_levels + j
            at = (i * own_levels + j) * stack
            for v in range(2):
                terms = pf_ref[q, v] * fields[at:at + stack]
                inc = terms[0:rows]
                for k in range(1, members):
                    inc = inc + terms[k * rows:(k + 1) * rows]
                inc_ref[d, v, j] = inc
        if d:
            remote(inc_ref.at[d], rs_ref.at[d - 1], rsr, scatter_sem, (source(d), band)).start()
    settle()
    pltpu.make_async_copy(rs_ref, rs_ref, rsr).wait()
    result = inc_ref[0]
    for d in range(1, n):
        result = result + rs_ref[d - 1]
    out_ref[...] = result
    pltpu.make_async_copy(rs_ref, rs_ref, pool.at[scatter_sem]).wait()


def write_out(u_ref, inc_ref, upd_hbm, inc_hbm, sem):
    first = pltpu.make_async_copy(u_ref, upd_hbm, sem.at[0])
    second = pltpu.make_async_copy(inc_ref, inc_hbm, sem.at[1])
    first.start()
    second.start()
    first.wait()
    second.wait()


def on_device(gradient, perturbations, weights, lon_taps, lat_taps, lev_taps, level_order):
    n, bands = lax.axis_size("mem"), lax.axis_size("lat")
    members, levels, rows, lons = weights.shape
    radius = lat_taps.shape[0] // 2
    norm = 1.0 / math.sqrt(members * n - 1)
    full, rem, halo, edge = sizes(rows, radius)
    stack = members * rows
    vmem, dma = pltpu.VMEM, pltpu.SemaphoreType.DMA
    anywhere = pl.BlockSpec(memory_space=pl.ANY)
    in_vmem = pl.BlockSpec(memory_space=pltpu.VMEM)
    updated, increment = pl.pallas_call(
        functools.partial(kernel, n, bands, norm, radius, lev_taps.shape[0]),
        out_shape=(
            vmem(weights.shape, F32),
            vmem(gradient.shape, F32),
        ),
        in_specs=[anywhere] * 7,
        out_specs=(in_vmem, in_vmem),
        scratch_shapes=[
            vmem((n,) + gradient.shape, F32),
            vmem(perturbations.shape, BF16),
            vmem((levels, 2, stack, lons), F32),
            vmem(weights.shape, F32),
            vmem((2, members, levels, edge, lons), F32),
            vmem((members, levels, halo, lons), F32),
            vmem((levels, stack, lons), F32),
            vmem((2, levels, stack, lons), F32),
            vmem((members, levels, rows + halo, lons), F32),
            vmem(weights.shape, F32),
            vmem((n,) + gradient.shape, F32),
            vmem((n - 1,) + gradient.shape, F32),
            vmem((lons, lons), BF16),
            vmem((lons, lons), BF16),
            vmem((lons, lons), BF16),
            vmem((lons, lons), BF16),
            vmem((rows + halo, 3 * packed(rows)), BF16),
            vmem((rows + halo, 3 * packed(2 * rows)), BF16),
            vmem((rows, 3 * packed(rows + halo)), BF16),
            pltpu.SMEM(lon_taps.shape, F32),
            pltpu.SMEM(lat_taps.shape, F32),
            pltpu.SMEM(lev_taps.shape, F32),
            pltpu.SMEM(level_order.shape, jnp.int32),
            dma((max(9, n + levels + 1),)),
            pltpu.SemaphoreType.REGULAR((max(1, n.bit_length() - 2),)),
            dma((n - 1,)),
            dma((levels,)),
            dma((2,)),
            dma,
        ],
        compiler_params=pltpu.CompilerParams(collective_id=0, has_side_effects=True),
        name="step",
    )(gradient, perturbations, weights, lon_taps, lat_taps, lev_taps, level_order)
    return pl.pallas_call(
        write_out,
        out_shape=(
            jax.ShapeDtypeStruct(updated.shape, F32),
            jax.ShapeDtypeStruct(increment.shape, F32),
        ),
        in_specs=[in_vmem] * 2,
        out_specs=(anywhere, anywhere),
        scratch_shapes=[dma((2,))],
        name="write_out",
    )(
        pltpu.with_memory_space_constraint(updated, pltpu.VMEM),
        pltpu.with_memory_space_constraint(increment, pltpu.VMEM),
    )


def solution(mesh):
    in_specs = (
        P(None, "mem", "lat", None),
        P("mem", None, None, "lat", None),
        P("mem", None, "lat", None),
        P(),
        P(),
        P(),
        P(),
    )
    out_specs = (P("mem", None, "lat", None), P(None, "mem", "lat", None))
    return jax.shard_map(
        on_device, mesh=mesh, in_specs=in_specs, out_specs=out_specs, check_vma=False
    )
```

```python
import functools
import math

import jax
import jax.numpy as jnp
from jax import lax
from jax.experimental import pallas as pl
from jax.experimental.pallas import tpu as pltpu
from jax.sharding import PartitionSpec as P

STEP_RATE = 0.5
TILE = 8
PACK = 16
PARTS = 2
F32 = jnp.float32
BF16 = jnp.bfloat16


def partner(me, d, n):
    if n & (n - 1):
        return (me + d) % n
    result = 0
    bit = 1
    while bit < n:
        result = result + ((me // bit + d // bit) % 2) * bit
        bit *= 2
    return result


def split(x):
    high = x.astype(BF16)
    return high, (x - high.astype(F32)).astype(BF16)


def dot(a, b):
    return lax.dot_general(a, b, (((1,), (0,)), ((), ())), preferred_element_type=F32)


def filter_lon(x, c_hi, c_lo):
    high, low = split(x)
    both = dot(jnp.concatenate([high, low], axis=0), c_hi[...])
    return both[:x.shape[0]] + (both[x.shape[0]:] + dot(high, c_lo[...]))


def packed(rows):
    return -(-rows // PACK) * PACK


def stacked(x):
    pad = packed(x.shape[0]) - x.shape[0]
    if pad:
        x = jnp.concatenate([x, jnp.zeros((pad, x.shape[1]), F32)], axis=0)
    high, low = split(x)
    return jnp.concatenate([high, high, low], axis=0)


def iota(shape, axis):
    return lax.broadcasted_iota(jnp.int32, shape, axis)


def sizes(rows, radius):
    full = radius // TILE * TILE
    rem = radius - full
    if 2 * rem > TILE or 2 * radius > rows:
        raise NotImplementedError("radius")
    halo = 2 * full + (TILE if rem else 0)
    edge = full + (TILE if rem else 0)
    return full, rem, halo, edge


def kernel(
    n, bands, norm, radius, lev_width,
    g_hbm, p_hbm, w_hbm, lon_hbm, lat_hbm, lev_hbm, order_hbm,
    u_ref, out_ref,
    g_all, p_ref, pf_ref, w_ref, wn_ref, wh_ref, z_ref, zn_ref, acc_ref, f_ref, inc_ref, rs_ref,
    a_hi, a_lo, b_hi, b_lo, k_own, k_halo, k_fwd,
    lon_t, lat_t, lev_t, order,
    pool, known_sem, gr, zr, wr, rsr,
):
    me = lax.axis_index("mem")
    band = lax.axis_index("lat")
    members, _, levels, rows, lons = p_ref.shape
    own_levels = g_hbm.shape[1]
    width = 2 * radius + 1
    full, rem, halo, edge = sizes(rows, radius)
    stack = members * rows
    has_low, has_high = band > 0, band < bands - 1
    mesh_ids = pl.DeviceIdType.MESH

    free = list(range(pool.shape[0]))
    loads = [
        pltpu.make_async_copy(src, dst, pool.at[free.pop(0)])
        for i, (src, dst) in enumerate([
            (g_hbm, g_all.at[0]), (w_hbm, w_ref), (lon_hbm, lon_t), (order_hbm, order),
            (p_hbm, p_ref), (lev_hbm, lev_t), (lat_hbm, lat_t),
        ])
    ]
    g_in, w_in, lon_in, order_in, p_in, lev_in, lat_in = range(len(loads))
    for copy in loads:
        copy.start()

    barrier = pltpu.get_barrier_semaphore()
    cube = not n & (n - 1)
    direct = [d for d in range(1, n) if not cube or not d & (d - 1)]
    rounds = [[d for d in range(1, n) if not cube or bin(d).count("1") == hops]
              for hops in range(1, len(direct) + 1 if cube else 2)]
    arrival = [0] + [d for ds in rounds for d in ds]

    def greet(semaphore):
        for d in direct:
            pl.semaphore_signal(
                semaphore, inc=1, device_id=(partner(me, d, n), band), device_id_type=mesh_ids
            )

    greet(barrier)

    @pl.when(has_low)
    def _():
        pl.semaphore_signal(barrier, inc=1, device_id=(me, band - 1), device_id_type=mesh_ids)

    @pl.when(has_high)
    def _():
        pl.semaphore_signal(barrier, inc=1, device_id=(me, band + 1), device_id_type=mesh_ids)

    def source(d):
        return partner(me, d, n) if cube else (me + n - d) % n

    sent = []

    def remote(src, dst, recv_sem, sem, target):
        return pltpu.make_async_remote_copy(
            src_ref=src,
            dst_ref=dst,
            send_sem=pool.at[sem],
            recv_sem=recv_sem,
            device_id=target,
            device_id_type=mesh_ids,
        )

    def gather(d):
        sem = free.pop(0)
        copy = remote(g_all.at[0], g_all.at[d], gr.at[d - 1], sem, (partner(me, d, n), band))
        copy.start()
        sent.append((sem, copy.wait_send))
        return copy

    odd = band % 2
    far_then_near = ((1 - odd, band - 1 + 2 * odd), (odd, band + 1 - 2 * odd))
    both = has_low & has_high
    one = has_low ^ has_high

    def to_bands(pairs, piece, whole, recv_sem):
        sem = free.pop(0)
        for side, target in pairs:
            @pl.when((target >= 0) & (target < bands))
            def _():
                remote(*piece(side), recv_sem, sem, (me, target)).start()

        def wait(semaphore):
            for count, here in ((2, both), (1, one)):
                ref = whole(count)
                pl.when(here)(pltpu.make_async_copy(ref, ref, semaphore).wait)

        sent.append((sem, lambda: wait(pool.at[sem])))
        return lambda: wait(recv_sem)

    def send_weights(size, low, high, recv_sem):
        at = ((low, low - rows + edge), (high, high))
        return to_bands(
            ((0, band + 1), (1, band - 1)),
            lambda side: (
                w_ref.at[:, :, at[side][0]:at[side][0] + size, :],
                wn_ref.at[side, :, :, at[side][1]:at[side][1] + size, :],
            ),
            lambda count: wn_ref.at[0:count, :, :, 0:size, :],
            recv_sem,
        )

    def settle(keep=0):
        for sem, wait in sent[:len(sent) - keep]:
            wait()
            free.append(sem)
        del sent[:len(sent) - keep]

    def loaded(i):
        loads[i].wait()
        free.append(i)

    loaded(g_in)
    neighbours = has_low.astype(jnp.int32) + has_high.astype(jnp.int32)
    pl.semaphore_wait(barrier, len(direct) + neighbours)
    if len(rounds) > 1:
        greet(known_sem.at[0])
    gathers = {d: gather(d) for d in rounds[0]}
    loaded(w_in)
    w_arrival = [send_weights(full, rows - full, 0, wr.at[0])]
    if rem:
        w_arrival.append(send_weights(rem, rows - radius, full, wr.at[1]))

    row, col = iota((TILE, lons), 0), iota((TILE, lons), 1)

    def lon_matrix(c_hi, c_lo, sign):
        off = sign * (col - row) + radius
        off = jnp.where(off < 0, off + lons, off)
        off = jnp.where(off >= lons, off - lons, off)
        base = jnp.zeros((TILE, lons), F32)
        for j in range(width):
            base = jnp.where(off == j, lon_t[j], base)
        for i in range(0, lons, PACK):
            value = jnp.concatenate(
                [pltpu.roll(base, i, 1) if i else base, pltpu.roll(base, i + TILE, 1)], axis=0
            )
            c_hi[i:i + PACK], c_lo[i:i + PACK] = split(value)

    loaded(lon_in)
    lon_matrix(a_hi, a_lo, 1)
    loaded(order_in)
    level_of = [
        order[source(q // own_levels) * own_levels + q % own_levels] for q in range(levels)
    ]
    loaded(p_in)

    def scaled(q):
        for v in range(2):
            for k in range(members):
                pf_ref[q, v, k * rows:(k + 1) * rows] = p_ref[k, v, level_of[q]].astype(F32) * norm

    z_arrival = {}
    ordered = [d * own_levels + j for d in arrival for j in range(own_levels)]
    parts = math.gcd(PARTS, members)

    def send_level(q):
        d, j = divmod(q, own_levels)
        g0 = jnp.concatenate([g_all[d, 0, j]] * members, axis=0)
        g1 = jnp.concatenate([g_all[d, 1, j]] * members, axis=0)
        z_ref[q] = filter_lon(pf_ref[q, 0] * g0 + pf_ref[q, 1] * g1, a_hi, a_lo)
        size = stack // parts if q == ordered[-1] else stack
        z_arrival[q] = [
            to_bands(
                far_then_near,
                lambda side, at=at: (z_ref.at[q, at:at + size], zn_ref.at[side, q, at:at + size]),
                lambda count, at=at: zn_ref.at[0:count, q, at:at + size],
                zr.at[levels + i - 1 if i else q],
            )
            for i, at in enumerate(range(0, stack, size))
        ]

    for j in range(own_levels):
        scaled(j)
        send_level(j)
    for i in range(1, len(rounds)):
        pl.semaphore_wait(known_sem.at[i - 1], len(direct))
        if i + 1 < len(rounds):
            greet(known_sem.at[i])
        gathers.update({d: gather(d) for d in rounds[i]})

    for q in range(own_levels, levels):
        scaled(q)
    for side, present in ((0, has_low), (1, has_high)):
        @pl.when(jnp.logical_not(present))
        def _():
            for q in range(levels):
                zn_ref[side, q] = jnp.zeros((stack, lons), F32)
            wn_ref[side] = jnp.zeros(wn_ref.shape[1:], F32)

    lon_matrix(b_hi, b_lo, -1)
    loaded(lat_in)

    def thirds(shape):
        c, size = iota(shape, 1), shape[1] // 3
        third = (c >= size).astype(jnp.int32) + (c >= 2 * size).astype(jnp.int32)
        return third, c - third * size

    def halo_pos(h):
        s = h - 2 * full
        rest = jnp.where(s < rem, rows + full + s, s - full - TILE)
        rest = jnp.where((s >= rem) & (s < TILE - rem), -4 * rows, rest)
        return jnp.where(h < full, h - full, jnp.where(h < 2 * full, rows + h - full, rest))

    def lat_matrix(out_pos, in_pos, third, sign):
        shift = sign * (in_pos - out_pos)
        value = jnp.zeros(shift.shape, F32)
        for j in range(width):
            value = jnp.where(shift == j - radius, lat_t[j], value)
        high = value.astype(BF16).astype(F32)
        return jnp.where(third == 1, value - high, high).astype(BF16)

    far = 8 * rows
    for k_ref, is_own in ((k_own, True), (k_halo, False)):
        r = iota(k_ref.shape, 0)
        third, c = thirds(k_ref.shape)
        if is_own:
            in_pos = jnp.where(c < rows, c, far)
        else:
            in_pos = jnp.where(c < rows, c - rows, jnp.where(c < 2 * rows, c, far))
        out_pos = jnp.where(r < rows, r, halo_pos(r - rows))
        k_ref[...] = lat_matrix(out_pos, in_pos, third, -1)
    third, c = thirds(k_fwd.shape)
    in_pos = jnp.where(c < rows, c, halo_pos(c - rows))
    inside = (in_pos + band * rows >= 0) & (in_pos + band * rows < bands * rows)
    inside = inside & (c < rows + halo)
    k_fwd[...] = lat_matrix(iota(k_fwd.shape, 0), jnp.where(inside, in_pos, far), third, 1)

    loaded(lev_in)
    coef = []
    for l in range(levels):
        coef.append([])
        for q in range(levels):
            tap = l - level_of[q] + lev_width // 2
            inside = (tap >= 0) & (tap < lev_width)
            value = lev_t[jnp.clip(tap, 0, lev_width - 1)]
            coef[l].append(jnp.where(inside, value, 0.0))

    for d in arrival[1:]:
        gathers[d].wait_recv()
        for j in range(own_levels):
            send_level(d * own_levels + j)

    for wait in w_arrival:
        wait()
    s = iota((TILE, lons), 0)
    for k in range(members):
        at = slice(k * rows, (k + 1) * rows)
        for l in range(levels):
            wh_ref[k, l, 0:full] = wn_ref[0, k, l, edge - full:edge]
            wh_ref[k, l, full:2 * full] = wn_ref[1, k, l, 0:full]
            if rem:
                wh_ref[k, l, 2 * full:halo] = jnp.where(
                    s < rem, wn_ref[1, k, l, full:edge], wn_ref[0, k, l, 0:TILE]
                )
        own = [dot(k_own[...], stacked(z_ref[q, at])) for q in range(levels)]
        for l in range(levels):
            total = jnp.concatenate([w_ref[k, l], wh_ref[k, l]], axis=0)
            for q in range(levels):
                total = total + coef[l][q] * own[q]
            acc_ref[k, l] = total

    for q in ordered[:-1]:
        z_arrival[q][0]()
        for k in range(members):
            at = slice(k * rows, (k + 1) * rows)
            y = dot(k_halo[...], stacked(jnp.concatenate([zn_ref[0, q, at], zn_ref[1, q, at]], axis=0)))
            for l in range(levels):
                acc_ref[k, l] = acc_ref[k, l] + coef[l][q] * y

    settle(keep=parts)
    q = ordered[-1]
    for i in range(parts):
        z_arrival[q][i]()
        group = range(i * members // parts, (i + 1) * members // parts)
        last = {}
        for k in group:
            at = slice(k * rows, (k + 1) * rows)
            x = jnp.concatenate([zn_ref[0, q, at], zn_ref[1, q, at]], axis=0)
            last[k] = dot(k_halo[...], stacked(x))
        for k in group:
            for l in range(levels):
                w = jnp.concatenate([w_ref[k, l], wh_ref[k, l]], axis=0)
                total = acc_ref[k, l] + coef[l][q] * last[k]
                u = w - STEP_RATE * total / (1.0 + jnp.abs(total))
                u_ref[k, l] = u[0:rows]
                f_ref[k, l] = dot(k_fwd[...], stacked(u))

    fields = []
    for d in reversed(arrival):
        for j in range(own_levels):
            for k in range(members):
                field = coef[0][d * own_levels + j] * f_ref[k, 0]
                for l in range(1, levels):
                    field = field + coef[l][d * own_levels + j] * f_ref[k, l]
                fields.append(field)
    fields = filter_lon(jnp.concatenate(fields, axis=0), b_hi, b_lo)

    scatter_sem = free.pop(0)
    for i, d in enumerate(reversed(arrival)):
        for j in range(own_levels):
            q = d * own_levels + j
            at = (i * own_levels + j) * stack
            for v in range(2):
                terms = pf_ref[q, v] * fields[at:at + stack]
                inc = terms[0:rows]
                for k in range(1, members):
                    inc = inc + terms[k * rows:(k + 1) * rows]
                inc_ref[d, v, j] = inc
        if d:
            remote(inc_ref.at[d], rs_ref.at[d - 1], rsr, scatter_sem, (source(d), band)).start()
    settle()
    pltpu.make_async_copy(rs_ref, rs_ref, rsr).wait()
    result = inc_ref[0]
    for d in range(1, n):
        result = result + rs_ref[d - 1]
    out_ref[...] = result
    pltpu.make_async_copy(rs_ref, rs_ref, pool.at[scatter_sem]).wait()


def write_out(u_ref, inc_ref, upd_hbm, inc_hbm, sem):
    first = pltpu.make_async_copy(u_ref, upd_hbm, sem.at[0])
    second = pltpu.make_async_copy(inc_ref, inc_hbm, sem.at[1])
    first.start()
    second.start()
    first.wait()
    second.wait()


def on_device(gradient, perturbations, weights, lon_taps, lat_taps, lev_taps, level_order):
    n, bands = lax.axis_size("mem"), lax.axis_size("lat")
    members, levels, rows, lons = weights.shape
    radius = lat_taps.shape[0] // 2
    norm = 1.0 / math.sqrt(members * n - 1)
    full, rem, halo, edge = sizes(rows, radius)
    stack = members * rows
    vmem, dma = pltpu.VMEM, pltpu.SemaphoreType.DMA
    anywhere = pl.BlockSpec(memory_space=pl.ANY)
    in_vmem = pl.BlockSpec(memory_space=pltpu.VMEM)
    updated, increment = pl.pallas_call(
        functools.partial(kernel, n, bands, norm, radius, lev_taps.shape[0]),
        out_shape=(
            vmem(weights.shape, F32),
            vmem(gradient.shape, F32),
        ),
        in_specs=[anywhere] * 7,
        out_specs=(in_vmem, in_vmem),
        scratch_shapes=[
            vmem((n,) + gradient.shape, F32),
            vmem(perturbations.shape, BF16),
            vmem((levels, 2, stack, lons), F32),
            vmem(weights.shape, F32),
            vmem((2, members, levels, edge, lons), F32),
            vmem((members, levels, halo, lons), F32),
            vmem((levels, stack, lons), F32),
            vmem((2, levels, stack, lons), F32),
            vmem((members, levels, rows + halo, lons), F32),
            vmem(weights.shape, F32),
            vmem((n,) + gradient.shape, F32),
            vmem((n - 1,) + gradient.shape, F32),
            vmem((lons, lons), BF16),
            vmem((lons, lons), BF16),
            vmem((lons, lons), BF16),
            vmem((lons, lons), BF16),
            vmem((rows + halo, 3 * packed(rows)), BF16),
            vmem((rows + halo, 3 * packed(2 * rows)), BF16),
            vmem((rows, 3 * packed(rows + halo)), BF16),
            pltpu.SMEM(lon_taps.shape, F32),
            pltpu.SMEM(lat_taps.shape, F32),
            pltpu.SMEM(lev_taps.shape, F32),
            pltpu.SMEM(level_order.shape, jnp.int32),
            dma((max(9, n + levels + 1) + math.gcd(PARTS, members) - 1,)),
            pltpu.SemaphoreType.REGULAR((max(1, n.bit_length() - 2),)),
            dma((n - 1,)),
            dma((levels + math.gcd(PARTS, members) - 1,)),
            dma((2,)),
            dma,
        ],
        compiler_params=pltpu.CompilerParams(collective_id=0, has_side_effects=True),
        name="step",
    )(gradient, perturbations, weights, lon_taps, lat_taps, lev_taps, level_order)
    return pl.pallas_call(
        write_out,
        out_shape=(
            jax.ShapeDtypeStruct(updated.shape, F32),
            jax.ShapeDtypeStruct(increment.shape, F32),
        ),
        in_specs=[in_vmem] * 2,
        out_specs=(anywhere, anywhere),
        scratch_shapes=[dma((2,))],
        name="write_out",
    )(
        pltpu.with_memory_space_constraint(updated, pltpu.VMEM),
        pltpu.with_memory_space_constraint(increment, pltpu.VMEM),
    )


def solution(mesh):
    in_specs = (
        P(None, "mem", "lat", None),
        P("mem", None, None, "lat", None),
        P("mem", None, "lat", None),
        P(),
        P(),
        P(),
        P(),
    )
    out_specs = (P("mem", None, "lat", None), P(None, "mem", "lat", None))
    return jax.shard_map(
        on_device, mesh=mesh, in_specs=in_specs, out_specs=out_specs, check_vma=False
    )
```

```python
import functools
import math

import jax
import jax.numpy as jnp
from jax import lax
from jax.experimental import pallas as pl
from jax.experimental.pallas import tpu as pltpu
from jax.sharding import PartitionSpec as P

STEP_RATE = 0.5
TILE = 8
PACK = 16
PARTS = 2
F32 = jnp.float32
BF16 = jnp.bfloat16


def partner(me, d, n):
    if n & (n - 1):
        return (me + d) % n
    result = 0
    bit = 1
    while bit < n:
        result = result + ((me // bit + d // bit) % 2) * bit
        bit *= 2
    return result


def split(x):
    high = x.astype(BF16)
    return high, (x - high.astype(F32)).astype(BF16)


def dot(a, b):
    return lax.dot_general(a, b, (((1,), (0,)), ((), ())), preferred_element_type=F32)


def filter_lon(x, c_hi, c_lo):
    high, low = split(x)
    both = dot(jnp.concatenate([high, low], axis=0), c_hi[...])
    return both[:x.shape[0]] + (both[x.shape[0]:] + dot(high, c_lo[...]))


def packed(rows):
    return -(-rows // PACK) * PACK


def stacked(x):
    pad = packed(x.shape[0]) - x.shape[0]
    if pad:
        x = jnp.concatenate([x, jnp.zeros((pad, x.shape[1]), F32)], axis=0)
    high, low = split(x)
    return jnp.concatenate([high, high, low], axis=0)


def iota(shape, axis):
    return lax.broadcasted_iota(jnp.int32, shape, axis)


def sizes(rows, radius):
    full = radius // TILE * TILE
    rem = radius - full
    if 2 * rem > TILE or 2 * radius > rows:
        raise NotImplementedError("radius")
    halo = 2 * full + (TILE if rem else 0)
    edge = full + (TILE if rem else 0)
    return full, rem, halo, edge


def kernel(
    n, bands, norm, radius, lev_width,
    g_hbm, p_hbm, w_hbm, lon_hbm, lat_hbm, lev_hbm, order_hbm,
    u_ref, out_ref,
    g_all, p_ref, pf_ref, w_ref, wn_ref, wh_ref, x_ref, z_ref, zn_ref, acc_ref, f_ref, inc_ref, rs_ref,
    a_hi, a_lo, b_hi, b_lo, k_own, k_halo, k_fwd,
    lon_t, lat_t, lev_t, order,
    pool, known_sem, gr, zr, wr, rsr,
):
    me = lax.axis_index("mem")
    band = lax.axis_index("lat")
    members, _, levels, rows, lons = p_ref.shape
    own_levels = g_hbm.shape[1]
    width = 2 * radius + 1
    full, rem, halo, edge = sizes(rows, radius)
    stack = members * rows
    has_low, has_high = band > 0, band < bands - 1
    mesh_ids = pl.DeviceIdType.MESH

    free = list(range(pool.shape[0]))
    loads = [
        pltpu.make_async_copy(src, dst, pool.at[free.pop(0)])
        for i, (src, dst) in enumerate([
            (g_hbm, g_all.at[0]), (w_hbm, w_ref), (lon_hbm, lon_t), (order_hbm, order),
            (p_hbm, p_ref), (lev_hbm, lev_t), (lat_hbm, lat_t),
        ])
    ]
    g_in, w_in, lon_in, order_in, p_in, lev_in, lat_in = range(len(loads))
    for copy in loads:
        copy.start()

    barrier = pltpu.get_barrier_semaphore()
    cube = not n & (n - 1)
    direct = [d for d in range(1, n) if not cube or not d & (d - 1)]
    rounds = [[d for d in range(1, n) if not cube or bin(d).count("1") == hops]
              for hops in range(1, len(direct) + 1 if cube else 2)]
    arrival = [0] + [d for ds in rounds for d in ds]

    def greet(semaphore):
        for d in direct:
            pl.semaphore_signal(
                semaphore, inc=1, device_id=(partner(me, d, n), band), device_id_type=mesh_ids
            )

    greet(barrier)

    @pl.when(has_low)
    def _():
        pl.semaphore_signal(barrier, inc=1, device_id=(me, band - 1), device_id_type=mesh_ids)

    @pl.when(has_high)
    def _():
        pl.semaphore_signal(barrier, inc=1, device_id=(me, band + 1), device_id_type=mesh_ids)

    def source(d):
        return partner(me, d, n) if cube else (me + n - d) % n

    sent = []

    def remote(src, dst, recv_sem, sem, target):
        return pltpu.make_async_remote_copy(
            src_ref=src,
            dst_ref=dst,
            send_sem=pool.at[sem],
            recv_sem=recv_sem,
            device_id=target,
            device_id_type=mesh_ids,
        )

    def gather(d):
        sem = free.pop(0)
        copy = remote(g_all.at[0], g_all.at[d], gr.at[d - 1], sem, (partner(me, d, n), band))
        copy.start()
        sent.append((sem, copy.wait_send))
        return copy

    odd = band % 2
    far_then_near = ((1 - odd, band - 1 + 2 * odd), (odd, band + 1 - 2 * odd))
    both = has_low & has_high
    one = has_low ^ has_high

    def to_bands(pairs, piece, whole, recv_sem):
        sem = free.pop(0)
        for side, target in pairs:
            @pl.when((target >= 0) & (target < bands))
            def _():
                remote(*piece(side), recv_sem, sem, (me, target)).start()

        def wait(semaphore):
            for count, here in ((2, both), (1, one)):
                ref = whole(count)
                pl.when(here)(pltpu.make_async_copy(ref, ref, semaphore).wait)

        sent.append((sem, lambda: wait(pool.at[sem])))
        return lambda: wait(recv_sem)

    def send_weights(size, low, high, recv_sem):
        at = ((low, low - rows + edge), (high, high))
        return to_bands(
            ((0, band + 1), (1, band - 1)),
            lambda side: (
                w_ref.at[:, :, at[side][0]:at[side][0] + size, :],
                wn_ref.at[side, :, :, at[side][1]:at[side][1] + size, :],
            ),
            lambda count: wn_ref.at[0:count, :, :, 0:size, :],
            recv_sem,
        )

    def settle(keep=0):
        for sem, wait in sent[:len(sent) - keep]:
            wait()
            free.append(sem)
        del sent[:len(sent) - keep]

    def loaded(i):
        loads[i].wait()
        free.append(i)

    loaded(g_in)
    neighbours = has_low.astype(jnp.int32) + has_high.astype(jnp.int32)
    pl.semaphore_wait(barrier, len(direct) + neighbours)
    if len(rounds) > 1:
        greet(known_sem.at[0])
    gathers = {d: gather(d) for d in rounds[0]}
    loaded(w_in)
    w_arrival = [send_weights(full, rows - full, 0, wr.at[0])]
    if rem:
        w_arrival.append(send_weights(rem, rows - radius, full, wr.at[1]))

    row, col = iota((TILE, lons), 0), iota((TILE, lons), 1)

    def lon_matrix(c_hi, c_lo, sign):
        off = sign * (col - row) + radius
        off = jnp.where(off < 0, off + lons, off)
        off = jnp.where(off >= lons, off - lons, off)
        base = jnp.zeros((TILE, lons), F32)
        for j in range(width):
            base = jnp.where(off == j, lon_t[j], base)
        for i in range(0, lons, PACK):
            value = jnp.concatenate(
                [pltpu.roll(base, i, 1) if i else base, pltpu.roll(base, i + TILE, 1)], axis=0
            )
            c_hi[i:i + PACK], c_lo[i:i + PACK] = split(value)

    loaded(lon_in)
    lon_matrix(a_hi, a_lo, 1)
    loaded(order_in)
    level_of = [
        order[source(q // own_levels) * own_levels + q % own_levels] for q in range(levels)
    ]
    loaded(p_in)

    def scaled(q):
        for v in range(2):
            for k in range(members):
                pf_ref[q, v, k * rows:(k + 1) * rows] = p_ref[k, v, level_of[q]].astype(F32) * norm

    z_arrival = {}
    ordered = [d * own_levels + j for d in arrival for j in range(own_levels)]
    parts = math.gcd(PARTS, members)
    unfiltered = ordered[own_levels:min(2 * own_levels, levels - 1)]

    def send_level(q):
        d, j = divmod(q, own_levels)
        g0 = jnp.concatenate([g_all[d, 0, j]] * members, axis=0)
        g1 = jnp.concatenate([g_all[d, 1, j]] * members, axis=0)
        x = pf_ref[q, 0] * g0 + pf_ref[q, 1] * g1
        src = z_ref.at[q]
        if q in unfiltered:
            src = x_ref.at[j]
            x_ref[j] = x
        else:
            z_ref[q] = filter_lon(x, a_hi, a_lo)
        size = stack // parts if q == ordered[-1] else stack
        z_arrival[q] = [
            to_bands(
                far_then_near,
                lambda side, at=at: (src.at[at:at + size], zn_ref.at[side, q, at:at + size]),
                lambda count, at=at: zn_ref.at[0:count, q, at:at + size],
                zr.at[levels + i - 1 if i else q],
            )
            for i, at in enumerate(range(0, stack, size))
        ]
        if q in unfiltered:
            z_ref[q] = filter_lon(x, a_hi, a_lo)

    for j in range(own_levels):
        scaled(j)
        send_level(j)
    for i in range(1, len(rounds)):
        pl.semaphore_wait(known_sem.at[i - 1], len(direct))
        if i + 1 < len(rounds):
            greet(known_sem.at[i])
        gathers.update({d: gather(d) for d in rounds[i]})

    for q in range(own_levels, levels):
        scaled(q)
    for side, present in ((0, has_low), (1, has_high)):
        @pl.when(jnp.logical_not(present))
        def _():
            for q in range(levels):
                zn_ref[side, q] = jnp.zeros((stack, lons), F32)
            wn_ref[side] = jnp.zeros(wn_ref.shape[1:], F32)

    lon_matrix(b_hi, b_lo, -1)
    loaded(lat_in)

    def thirds(shape):
        c, size = iota(shape, 1), shape[1] // 3
        third = (c >= size).astype(jnp.int32) + (c >= 2 * size).astype(jnp.int32)
        return third, c - third * size

    def halo_pos(h):
        s = h - 2 * full
        rest = jnp.where(s < rem, rows + full + s, s - full - TILE)
        rest = jnp.where((s >= rem) & (s < TILE - rem), -4 * rows, rest)
        return jnp.where(h < full, h - full, jnp.where(h < 2 * full, rows + h - full, rest))

    def lat_matrix(out_pos, in_pos, third, sign):
        shift = sign * (in_pos - out_pos)
        value = jnp.zeros(shift.shape, F32)
        for j in range(width):
            value = jnp.where(shift == j - radius, lat_t[j], value)
        high = value.astype(BF16).astype(F32)
        return jnp.where(third == 1, value - high, high).astype(BF16)

    far = 8 * rows
    for k_ref, is_own in ((k_own, True), (k_halo, False)):
        r = iota(k_ref.shape, 0)
        third, c = thirds(k_ref.shape)
        if is_own:
            in_pos = jnp.where(c < rows, c, far)
        else:
            in_pos = jnp.where(c < rows, c - rows, jnp.where(c < 2 * rows, c, far))
        out_pos = jnp.where(r < rows, r, halo_pos(r - rows))
        k_ref[...] = lat_matrix(out_pos, in_pos, third, -1)
    third, c = thirds(k_fwd.shape)
    in_pos = jnp.where(c < rows, c, halo_pos(c - rows))
    inside = (in_pos + band * rows >= 0) & (in_pos + band * rows < bands * rows)
    inside = inside & (c < rows + halo)
    k_fwd[...] = lat_matrix(iota(k_fwd.shape, 0), jnp.where(inside, in_pos, far), third, 1)

    loaded(lev_in)
    coef = []
    for l in range(levels):
        coef.append([])
        for q in range(levels):
            tap = l - level_of[q] + lev_width // 2
            inside = (tap >= 0) & (tap < lev_width)
            value = lev_t[jnp.clip(tap, 0, lev_width - 1)]
            coef[l].append(jnp.where(inside, value, 0.0))

    for d in arrival[1:]:
        gathers[d].wait_recv()
        for j in range(own_levels):
            send_level(d * own_levels + j)

    for wait in w_arrival:
        wait()
    s = iota((TILE, lons), 0)
    for k in range(members):
        at = slice(k * rows, (k + 1) * rows)
        for l in range(levels):
            wh_ref[k, l, 0:full] = wn_ref[0, k, l, edge - full:edge]
            wh_ref[k, l, full:2 * full] = wn_ref[1, k, l, 0:full]
            if rem:
                wh_ref[k, l, 2 * full:halo] = jnp.where(
                    s < rem, wn_ref[1, k, l, full:edge], wn_ref[0, k, l, 0:TILE]
                )
        own = [dot(k_own[...], stacked(z_ref[q, at])) for q in range(levels)]
        for l in range(levels):
            total = jnp.concatenate([w_ref[k, l], wh_ref[k, l]], axis=0)
            for q in range(levels):
                total = total + coef[l][q] * own[q]
            acc_ref[k, l] = total

    for q in ordered[:-1]:
        z_arrival[q][0]()
        if q in unfiltered:
            z = filter_lon(jnp.concatenate([zn_ref[0, q], zn_ref[1, q]], axis=0), a_hi, a_lo)
            zn_ref[0, q], zn_ref[1, q] = z[:stack], z[stack:]
        for k in range(members):
            at = slice(k * rows, (k + 1) * rows)
            y = dot(k_halo[...], stacked(jnp.concatenate([zn_ref[0, q, at], zn_ref[1, q, at]], axis=0)))
            for l in range(levels):
                acc_ref[k, l] = acc_ref[k, l] + coef[l][q] * y

    settle(keep=parts)
    q = ordered[-1]
    for i in range(parts):
        z_arrival[q][i]()
        group = range(i * members // parts, (i + 1) * members // parts)
        last = {}
        for k in group:
            at = slice(k * rows, (k + 1) * rows)
            x = jnp.concatenate([zn_ref[0, q, at], zn_ref[1, q, at]], axis=0)
            last[k] = dot(k_halo[...], stacked(x))
        for k in group:
            for l in range(levels):
                w = jnp.concatenate([w_ref[k, l], wh_ref[k, l]], axis=0)
                total = acc_ref[k, l] + coef[l][q] * last[k]
                u = w - STEP_RATE * total / (1.0 + jnp.abs(total))
                u_ref[k, l] = u[0:rows]
                f_ref[k, l] = dot(k_fwd[...], stacked(u))

    scatter_sem = free.pop(0)
    backward = arrival[::-1]
    for group in (backward[:2], backward[2:]):
        order_q = [d * own_levels + j for d in group for j in range(own_levels)]
        fields = []
        for q in order_q:
            for k in range(members):
                field = coef[0][q] * f_ref[k, 0]
                for l in range(1, levels):
                    field = field + coef[l][q] * f_ref[k, l]
                fields.append(field)
        fields = filter_lon(jnp.concatenate(fields, axis=0), b_hi, b_lo)
        for i, q in enumerate(order_q):
            for v in range(2):
                terms = pf_ref[q, v] * fields[i * stack:(i + 1) * stack]
                inc = terms[0:rows]
                for k in range(1, members):
                    inc = inc + terms[k * rows:(k + 1) * rows]
                inc_ref[q // own_levels, v, q % own_levels] = inc
            d = q // own_levels
            if d and (q + 1) % own_levels == 0:
                remote(inc_ref.at[d], rs_ref.at[d - 1], rsr, scatter_sem, (source(d), band)).start()
    settle()
    pltpu.make_async_copy(rs_ref, rs_ref, rsr).wait()
    result = inc_ref[0]
    for d in range(1, n):
        result = result + rs_ref[d - 1]
    out_ref[...] = result
    pltpu.make_async_copy(rs_ref, rs_ref, pool.at[scatter_sem]).wait()


def write_out(u_ref, inc_ref, upd_hbm, inc_hbm, sem):
    first = pltpu.make_async_copy(u_ref, upd_hbm, sem.at[0])
    second = pltpu.make_async_copy(inc_ref, inc_hbm, sem.at[1])
    first.start()
    second.start()
    first.wait()
    second.wait()


def on_device(gradient, perturbations, weights, lon_taps, lat_taps, lev_taps, level_order):
    n, bands = lax.axis_size("mem"), lax.axis_size("lat")
    members, levels, rows, lons = weights.shape
    radius = lat_taps.shape[0] // 2
    norm = 1.0 / math.sqrt(members * n - 1)
    full, rem, halo, edge = sizes(rows, radius)
    stack = members * rows
    vmem, dma = pltpu.VMEM, pltpu.SemaphoreType.DMA
    anywhere = pl.BlockSpec(memory_space=pl.ANY)
    in_vmem = pl.BlockSpec(memory_space=pltpu.VMEM)
    updated, increment = pl.pallas_call(
        functools.partial(kernel, n, bands, norm, radius, lev_taps.shape[0]),
        out_shape=(
            vmem(weights.shape, F32),
            vmem(gradient.shape, F32),
        ),
        in_specs=[anywhere] * 7,
        out_specs=(in_vmem, in_vmem),
        scratch_shapes=[
            vmem((n,) + gradient.shape, F32),
            vmem(perturbations.shape, BF16),
            vmem((levels, 2, stack, lons), F32),
            vmem(weights.shape, F32),
            vmem((2, members, levels, edge, lons), F32),
            vmem((members, levels, halo, lons), F32),
            vmem((gradient.shape[1], stack, lons), F32),
            vmem((levels, stack, lons), F32),
            vmem((2, levels, stack, lons), F32),
            vmem((members, levels, rows + halo, lons), F32),
            vmem(weights.shape, F32),
            vmem((n,) + gradient.shape, F32),
            vmem((n - 1,) + gradient.shape, F32),
            vmem((lons, lons), BF16),
            vmem((lons, lons), BF16),
            vmem((lons, lons), BF16),
            vmem((lons, lons), BF16),
            vmem((rows + halo, 3 * packed(rows)), BF16),
            vmem((rows + halo, 3 * packed(2 * rows)), BF16),
            vmem((rows, 3 * packed(rows + halo)), BF16),
            pltpu.SMEM(lon_taps.shape, F32),
            pltpu.SMEM(lat_taps.shape, F32),
            pltpu.SMEM(lev_taps.shape, F32),
            pltpu.SMEM(level_order.shape, jnp.int32),
            dma((max(9, n + levels + 1) + math.gcd(PARTS, members) - 1,)),
            pltpu.SemaphoreType.REGULAR((max(1, n.bit_length() - 2),)),
            dma((n - 1,)),
            dma((levels + math.gcd(PARTS, members) - 1,)),
            dma((2,)),
            dma,
        ],
        compiler_params=pltpu.CompilerParams(collective_id=0, has_side_effects=True),
        name="step",
    )(gradient, perturbations, weights, lon_taps, lat_taps, lev_taps, level_order)
    return pl.pallas_call(
        write_out,
        out_shape=(
            jax.ShapeDtypeStruct(updated.shape, F32),
            jax.ShapeDtypeStruct(increment.shape, F32),
        ),
        in_specs=[in_vmem] * 2,
        out_specs=(anywhere, anywhere),
        scratch_shapes=[dma((2,))],
        name="write_out",
    )(
        pltpu.with_memory_space_constraint(updated, pltpu.VMEM),
        pltpu.with_memory_space_constraint(increment, pltpu.VMEM),
    )


def solution(mesh):
    in_specs = (
        P(None, "mem", "lat", None),
        P("mem", None, None, "lat", None),
        P("mem", None, "lat", None),
        P(),
        P(),
        P(),
        P(),
    )
    out_specs = (P("mem", None, "lat", None), P(None, "mem", "lat", None))
    return jax.shard_map(
        on_device, mesh=mesh, in_specs=in_specs, out_specs=out_specs, check_vma=False
    )
```

```python
import functools
import math

import jax
import jax.numpy as jnp
from jax import lax
from jax.experimental import pallas as pl
from jax.experimental.pallas import tpu as pltpu
from jax.sharding import PartitionSpec as P

STEP_RATE = 0.5
TILE = 8
PACK = 16
PARTS = 2
F32 = jnp.float32
BF16 = jnp.bfloat16


def partner(me, d, n):
    if n & (n - 1):
        return (me + d) % n
    result = 0
    bit = 1
    while bit < n:
        result = result + ((me // bit + d // bit) % 2) * bit
        bit *= 2
    return result


def split(x):
    high = x.astype(BF16)
    return high, (x - high.astype(F32)).astype(BF16)


def dot(a, b):
    return lax.dot_general(a, b, (((1,), (0,)), ((), ())), preferred_element_type=F32)


def filter_lon(x, c_hi, c_lo):
    high, low = split(x)
    both = dot(jnp.concatenate([high, low], axis=0), c_hi[...])
    return both[:x.shape[0]] + (both[x.shape[0]:] + dot(high, c_lo[...]))


def packed(rows):
    return -(-rows // PACK) * PACK


def stacked(x):
    pad = packed(x.shape[0]) - x.shape[0]
    if pad:
        x = jnp.concatenate([x, jnp.zeros((pad, x.shape[1]), F32)], axis=0)
    high, low = split(x)
    return jnp.concatenate([high, high, low], axis=0)


def iota(shape, axis):
    return lax.broadcasted_iota(jnp.int32, shape, axis)


def sizes(rows, radius):
    full = radius // TILE * TILE
    rem = radius - full
    if 2 * rem > TILE or 2 * radius > rows:
        raise NotImplementedError("radius")
    halo = 2 * full + (TILE if rem else 0)
    edge = full + (TILE if rem else 0)
    return full, rem, halo, edge


def kernel(
    n, bands, norm, radius, lev_width,
    g_hbm, p_hbm, w_hbm, lon_hbm, lat_hbm, lev_hbm, order_hbm,
    u_ref, out_ref,
    g_all, p_ref, pf_ref, w_ref, wn_ref, wh_ref, x_ref, z_ref, zn_ref, acc_ref, f_ref, inc_ref, rs_ref,
    a_hi, a_lo, b_hi, b_lo, k_own, k_halo, k_fwd,
    lon_t, lat_t, lev_t, order,
    pool, known_sem, gr, zr, wr, rsr,
):
    me = lax.axis_index("mem")
    band = lax.axis_index("lat")
    members, _, levels, rows, lons = p_ref.shape
    own_levels = g_hbm.shape[1]
    width = 2 * radius + 1
    full, rem, halo, edge = sizes(rows, radius)
    stack = members * rows
    has_low, has_high = band > 0, band < bands - 1
    mesh_ids = pl.DeviceIdType.MESH

    free = list(range(pool.shape[0]))
    loads = [
        pltpu.make_async_copy(src, dst, pool.at[free.pop(0)])
        for i, (src, dst) in enumerate([
            (g_hbm, g_all.at[0]), (lon_hbm, lon_t), (order_hbm, order), (w_hbm, w_ref),
            (p_hbm, p_ref), (lev_hbm, lev_t), (lat_hbm, lat_t),
        ])
    ]
    g_in, lon_in, order_in, w_in, p_in, lev_in, lat_in = range(len(loads))
    for copy in loads:
        copy.start()

    barrier = pltpu.get_barrier_semaphore()
    cube = not n & (n - 1)
    direct = [d for d in range(1, n) if not cube or not d & (d - 1)]
    rounds = [[d for d in range(1, n) if not cube or bin(d).count("1") == hops]
              for hops in range(1, len(direct) + 1 if cube else 2)]
    arrival = [0] + [d for ds in rounds for d in ds]

    def greet(semaphore):
        for d in direct:
            pl.semaphore_signal(
                semaphore, inc=1, device_id=(partner(me, d, n), band), device_id_type=mesh_ids
            )

    greet(barrier)

    @pl.when(has_low)
    def _():
        pl.semaphore_signal(barrier, inc=1, device_id=(me, band - 1), device_id_type=mesh_ids)

    @pl.when(has_high)
    def _():
        pl.semaphore_signal(barrier, inc=1, device_id=(me, band + 1), device_id_type=mesh_ids)

    def source(d):
        return partner(me, d, n) if cube else (me + n - d) % n

    sent = []

    def remote(src, dst, recv_sem, sem, target):
        return pltpu.make_async_remote_copy(
            src_ref=src,
            dst_ref=dst,
            send_sem=pool.at[sem],
            recv_sem=recv_sem,
            device_id=target,
            device_id_type=mesh_ids,
        )

    def gather(d):
        sem = free.pop(0)
        copy = remote(g_all.at[0], g_all.at[d], gr.at[d - 1], sem, (partner(me, d, n), band))
        copy.start()
        sent.append((sem, copy.wait_send))
        return copy

    odd = band % 2
    far_then_near = ((1 - odd, band - 1 + 2 * odd, True), (odd, band + 1 - 2 * odd, True))
    both = has_low & has_high
    one = has_low ^ has_high

    def to_bands(pairs, piece, whole, recv_sem):
        sem = free.pop(0)
        for side, target, here in pairs:
            @pl.when((target >= 0) & (target < bands) & here)
            def _():
                remote(*piece(side), recv_sem, sem, (me, target)).start()

        def wait(semaphore):
            for count, here in ((2, both), (1, one)):
                ref = whole(count)
                pl.when(here)(pltpu.make_async_copy(ref, ref, semaphore).wait)

        sent.append((sem, lambda: wait(pool.at[sem])))
        return lambda: wait(recv_sem)

    def send_weights(size, low, high, recv_sem):
        at = ((low, low - rows + edge), (high, high))
        return to_bands(
            ((1, band - 1, odd == 0), (0, band + 1, True), (1, band - 1, odd == 1)),
            lambda side: (
                w_ref.at[:, :, at[side][0]:at[side][0] + size, :],
                wn_ref.at[side, :, :, at[side][1]:at[side][1] + size, :],
            ),
            lambda count: wn_ref.at[0:count, :, :, 0:size, :],
            recv_sem,
        )

    def settle(keep=0):
        for sem, wait in sent[:len(sent) - keep]:
            wait()
            free.append(sem)
        del sent[:len(sent) - keep]

    def loaded(i):
        loads[i].wait()
        free.append(i)

    loaded(g_in)
    loaded(lon_in)
    loaded(order_in)
    neighbours = has_low.astype(jnp.int32) + has_high.astype(jnp.int32)
    pl.semaphore_wait(barrier, len(direct) + neighbours)
    if len(rounds) > 1:
        greet(known_sem.at[0])
    gathers = {d: gather(d) for d in rounds[0]}
    loaded(w_in)
    w_arrival = [send_weights(full, rows - full, 0, wr.at[0])]
    if rem:
        w_arrival.append(send_weights(rem, rows - radius, full, wr.at[1]))

    row, col = iota((TILE, lons), 0), iota((TILE, lons), 1)

    def lon_matrix(c_hi, c_lo, sign):
        off = sign * (col - row) + radius
        off = jnp.where(off < 0, off + lons, off)
        off = jnp.where(off >= lons, off - lons, off)
        base = jnp.zeros((TILE, lons), F32)
        for j in range(width):
            base = jnp.where(off == j, lon_t[j], base)
        for i in range(0, lons, PACK):
            value = jnp.concatenate(
                [pltpu.roll(base, i, 1) if i else base, pltpu.roll(base, i + TILE, 1)], axis=0
            )
            c_hi[i:i + PACK], c_lo[i:i + PACK] = split(value)

    lon_matrix(a_hi, a_lo, 1)
    level_of = [
        order[source(q // own_levels) * own_levels + q % own_levels] for q in range(levels)
    ]
    loaded(p_in)

    def scaled(q):
        for v in range(2):
            for k in range(members):
                pf_ref[q, v, k * rows:(k + 1) * rows] = p_ref[k, v, level_of[q]].astype(F32) * norm

    z_arrival = {}
    ordered = [d * own_levels + j for d in arrival for j in range(own_levels)]
    parts = math.gcd(PARTS, members)
    unfiltered = ordered[own_levels:min(2 * own_levels, levels - 1)]

    def send_level(q):
        d, j = divmod(q, own_levels)
        g0 = jnp.concatenate([g_all[d, 0, j]] * members, axis=0)
        g1 = jnp.concatenate([g_all[d, 1, j]] * members, axis=0)
        x = pf_ref[q, 0] * g0 + pf_ref[q, 1] * g1
        src = z_ref.at[q]
        if q in unfiltered:
            src = x_ref.at[j]
            x_ref[j] = x
        else:
            z_ref[q] = filter_lon(x, a_hi, a_lo)
        size = stack // parts if q == ordered[-1] else stack
        z_arrival[q] = [
            to_bands(
                far_then_near,
                lambda side, at=at: (src.at[at:at + size], zn_ref.at[side, q, at:at + size]),
                lambda count, at=at: zn_ref.at[0:count, q, at:at + size],
                zr.at[levels + i - 1 if i else q],
            )
            for i, at in enumerate(range(0, stack, size))
        ]
        if q in unfiltered:
            z_ref[q] = filter_lon(x, a_hi, a_lo)

    early = len(sent)
    for j in range(own_levels):
        scaled(j)
        send_level(j)
    loaded(lev_in)
    loaded(lat_in)
    for i in range(1, len(rounds)):
        pl.semaphore_wait(known_sem.at[i - 1], len(direct))
        if i + 1 < len(rounds):
            greet(known_sem.at[i])
        gathers.update({d: gather(d) for d in rounds[i]})

    for q in range(own_levels, levels):
        scaled(q)
    for side, present in ((0, has_low), (1, has_high)):
        @pl.when(jnp.logical_not(present))
        def _():
            for q in range(levels):
                zn_ref[side, q] = jnp.zeros((stack, lons), F32)
            wn_ref[side] = jnp.zeros(wn_ref.shape[1:], F32)

    lon_matrix(b_hi, b_lo, -1)

    def thirds(shape):
        c, size = iota(shape, 1), shape[1] // 3
        third = (c >= size).astype(jnp.int32) + (c >= 2 * size).astype(jnp.int32)
        return third, c - third * size

    def halo_pos(h):
        s = h - 2 * full
        rest = jnp.where(s < rem, rows + full + s, s - full - TILE)
        rest = jnp.where((s >= rem) & (s < TILE - rem), -4 * rows, rest)
        return jnp.where(h < full, h - full, jnp.where(h < 2 * full, rows + h - full, rest))

    def lat_matrix(out_pos, in_pos, third, sign):
        shift = sign * (in_pos - out_pos)
        value = jnp.zeros(shift.shape, F32)
        for j in range(width):
            value = jnp.where(shift == j - radius, lat_t[j], value)
        high = value.astype(BF16).astype(F32)
        return jnp.where(third == 1, value - high, high).astype(BF16)

    far = 8 * rows
    for k_ref, is_own in ((k_own, True), (k_halo, False)):
        r = iota(k_ref.shape, 0)
        third, c = thirds(k_ref.shape)
        if is_own:
            in_pos = jnp.where(c < rows, c, far)
        else:
            in_pos = jnp.where(c < rows, c - rows, jnp.where(c < 2 * rows, c, far))
        out_pos = jnp.where(r < rows, r, halo_pos(r - rows))
        k_ref[...] = lat_matrix(out_pos, in_pos, third, -1)
    third, c = thirds(k_fwd.shape)
    in_pos = jnp.where(c < rows, c, halo_pos(c - rows))
    inside = (in_pos + band * rows >= 0) & (in_pos + band * rows < bands * rows)
    inside = inside & (c < rows + halo)
    k_fwd[...] = lat_matrix(iota(k_fwd.shape, 0), jnp.where(inside, in_pos, far), third, 1)

    coef = []
    for l in range(levels):
        coef.append([])
        for q in range(levels):
            tap = l - level_of[q] + lev_width // 2
            inside = (tap >= 0) & (tap < lev_width)
            value = lev_t[jnp.clip(tap, 0, lev_width - 1)]
            coef[l].append(jnp.where(inside, value, 0.0))

    for d in arrival[1:]:
        if d == arrival[2]:
            settle(keep=len(sent) - early)
        gathers[d].wait_recv()
        for j in range(own_levels):
            send_level(d * own_levels + j)

    for wait in w_arrival:
        wait()
    s = iota((TILE, lons), 0)
    for k in range(members):
        at = slice(k * rows, (k + 1) * rows)
        for l in range(levels):
            wh_ref[k, l, 0:full] = wn_ref[0, k, l, edge - full:edge]
            wh_ref[k, l, full:2 * full] = wn_ref[1, k, l, 0:full]
            if rem:
                wh_ref[k, l, 2 * full:halo] = jnp.where(
                    s < rem, wn_ref[1, k, l, full:edge], wn_ref[0, k, l, 0:TILE]
                )
        own = [dot(k_own[...], stacked(z_ref[q, at])) for q in range(levels)]
        for l in range(levels):
            total = jnp.concatenate([w_ref[k, l], wh_ref[k, l]], axis=0)
            for q in range(levels):
                total = total + coef[l][q] * own[q]
            acc_ref[k, l] = total

    for q in ordered[:-1]:
        z_arrival[q][0]()
        if q in unfiltered:
            z = filter_lon(jnp.concatenate([zn_ref[0, q], zn_ref[1, q]], axis=0), a_hi, a_lo)
            zn_ref[0, q], zn_ref[1, q] = z[:stack], z[stack:]
        for k in range(members):
            at = slice(k * rows, (k + 1) * rows)
            y = dot(k_halo[...], stacked(jnp.concatenate([zn_ref[0, q, at], zn_ref[1, q, at]], axis=0)))
            for l in range(levels):
                acc_ref[k, l] = acc_ref[k, l] + coef[l][q] * y

    settle(keep=parts)
    q = ordered[-1]
    for i in range(parts):
        z_arrival[q][i]()
        group = range(i * members // parts, (i + 1) * members // parts)
        last = {}
        for k in group:
            at = slice(k * rows, (k + 1) * rows)
            x = jnp.concatenate([zn_ref[0, q, at], zn_ref[1, q, at]], axis=0)
            last[k] = dot(k_halo[...], stacked(x))
        for k in group:
            for l in range(levels):
                w = jnp.concatenate([w_ref[k, l], wh_ref[k, l]], axis=0)
                total = acc_ref[k, l] + coef[l][q] * last[k]
                u = w - STEP_RATE * total / (1.0 + jnp.abs(total))
                u_ref[k, l] = u[0:rows]
                f_ref[k, l] = dot(k_fwd[...], stacked(u))

    scatter_sem = free.pop(0)
    backward = arrival[::-1]
    for group in (backward[0:3], backward[3:]):
        order_q = [d * own_levels + j for d in group for j in range(own_levels)]
        fields = []
        for q in order_q:
            for k in range(members):
                field = coef[0][q] * f_ref[k, 0]
                for l in range(1, levels):
                    field = field + coef[l][q] * f_ref[k, l]
                fields.append(field)
        fields = filter_lon(jnp.concatenate(fields, axis=0), b_hi, b_lo)
        for i, q in enumerate(order_q):
            for v in range(2):
                terms = pf_ref[q, v] * fields[i * stack:(i + 1) * stack]
                inc = terms[0:rows]
                for k in range(1, members):
                    inc = inc + terms[k * rows:(k + 1) * rows]
                inc_ref[q // own_levels, v, q % own_levels] = inc
            d = q // own_levels
            if d and (q + 1) % own_levels == 0:
                remote(inc_ref.at[d], rs_ref.at[d - 1], rsr, scatter_sem, (source(d), band)).start()
    settle()
    pltpu.make_async_copy(rs_ref, rs_ref, rsr).wait()
    result = inc_ref[0]
    for d in range(1, n):
        result = result + rs_ref[d - 1]
    out_ref[...] = result
    pltpu.make_async_copy(rs_ref, rs_ref, pool.at[scatter_sem]).wait()


def write_out(u_ref, inc_ref, upd_hbm, inc_hbm, sem):
    first = pltpu.make_async_copy(u_ref, upd_hbm, sem.at[0])
    second = pltpu.make_async_copy(inc_ref, inc_hbm, sem.at[1])
    first.start()
    second.start()
    first.wait()
    second.wait()


def on_device(gradient, perturbations, weights, lon_taps, lat_taps, lev_taps, level_order):
    n, bands = lax.axis_size("mem"), lax.axis_size("lat")
    members, levels, rows, lons = weights.shape
    radius = lat_taps.shape[0] // 2
    norm = 1.0 / math.sqrt(members * n - 1)
    full, rem, halo, edge = sizes(rows, radius)
    stack = members * rows
    vmem, dma = pltpu.VMEM, pltpu.SemaphoreType.DMA
    anywhere = pl.BlockSpec(memory_space=pl.ANY)
    in_vmem = pl.BlockSpec(memory_space=pltpu.VMEM)
    updated, increment = pl.pallas_call(
        functools.partial(kernel, n, bands, norm, radius, lev_taps.shape[0]),
        out_shape=(
            vmem(weights.shape, F32),
            vmem(gradient.shape, F32),
        ),
        in_specs=[anywhere] * 7,
        out_specs=(in_vmem, in_vmem),
        scratch_shapes=[
            vmem((n,) + gradient.shape, F32),
            vmem(perturbations.shape, BF16),
            vmem((levels, 2, stack, lons), F32),
            vmem(weights.shape, F32),
            vmem((2, members, levels, edge, lons), F32),
            vmem((members, levels, halo, lons), F32),
            vmem((gradient.shape[1], stack, lons), F32),
            vmem((levels, stack, lons), F32),
            vmem((2, levels, stack, lons), F32),
            vmem((members, levels, rows + halo, lons), F32),
            vmem(weights.shape, F32),
            vmem((n,) + gradient.shape, F32),
            vmem((n - 1,) + gradient.shape, F32),
            vmem((lons, lons), BF16),
            vmem((lons, lons), BF16),
            vmem((lons, lons), BF16),
            vmem((lons, lons), BF16),
            vmem((rows + halo, 3 * packed(rows)), BF16),
            vmem((rows + halo, 3 * packed(2 * rows)), BF16),
            vmem((rows, 3 * packed(rows + halo)), BF16),
            pltpu.SMEM(lon_taps.shape, F32),
            pltpu.SMEM(lat_taps.shape, F32),
            pltpu.SMEM(lev_taps.shape, F32),
            pltpu.SMEM(level_order.shape, jnp.int32),
            dma((max(7, n + levels - 1),)),
            pltpu.SemaphoreType.REGULAR((max(1, n.bit_length() - 2),)),
            dma((n - 1,)),
            dma((levels + math.gcd(PARTS, members) - 1,)),
            dma((2,)),
            dma,
        ],
        compiler_params=pltpu.CompilerParams(collective_id=0, has_side_effects=True),
        name="step",
    )(gradient, perturbations, weights, lon_taps, lat_taps, lev_taps, level_order)
    return pl.pallas_call(
        write_out,
        out_shape=(
            jax.ShapeDtypeStruct(updated.shape, F32),
            jax.ShapeDtypeStruct(increment.shape, F32),
        ),
        in_specs=[in_vmem] * 2,
        out_specs=(anywhere, anywhere),
        scratch_shapes=[dma((2,))],
        name="write_out",
    )(
        pltpu.with_memory_space_constraint(updated, pltpu.VMEM),
        pltpu.with_memory_space_constraint(increment, pltpu.VMEM),
    )


def solution(mesh):
    in_specs = (
        P(None, "mem", "lat", None),
        P("mem", None, None, "lat", None),
        P("mem", None, "lat", None),
        P(),
        P(),
        P(),
        P(),
    )
    out_specs = (P("mem", None, "lat", None), P(None, "mem", "lat", None))
    return jax.shard_map(
        on_device, mesh=mesh, in_specs=in_specs, out_specs=out_specs, check_vma=False
    )
```

```python
import functools
import math

import jax
import jax.numpy as jnp
from jax import lax
from jax.experimental import pallas as pl
from jax.experimental.pallas import tpu as pltpu
from jax.sharding import PartitionSpec as P

STEP_RATE = 0.5
TILE = 8
PACK = 16
PARTS = 2
F32 = jnp.float32
BF16 = jnp.bfloat16


def partner(me, d, n):
    if n & (n - 1):
        return (me + d) % n
    result = 0
    bit = 1
    while bit < n:
        result = result + ((me // bit + d // bit) % 2) * bit
        bit *= 2
    return result


def split(x):
    high = x.astype(BF16)
    return high, (x - high.astype(F32)).astype(BF16)


def dot(a, b):
    return lax.dot_general(a, b, (((1,), (0,)), ((), ())), preferred_element_type=F32)


def filter_split(high, low, c_hi, c_lo):
    size = high.shape[0]
    both = dot(jnp.concatenate([high, low], axis=0), c_hi[...])
    return both[:size] + (both[size:] + dot(high, c_lo[...]))


def filter_lon(x, c_hi, c_lo):
    return filter_split(*split(x), c_hi, c_lo)


def packed(rows):
    return -(-rows // PACK) * PACK


def stacked(x):
    pad = packed(x.shape[0]) - x.shape[0]
    if pad:
        x = jnp.concatenate([x, jnp.zeros((pad, x.shape[1]), F32)], axis=0)
    high, low = split(x)
    return jnp.concatenate([high, high, low], axis=0)


def iota(shape, axis):
    return lax.broadcasted_iota(jnp.int32, shape, axis)


def sizes(rows, radius):
    full = radius // TILE * TILE
    rem = radius - full
    if 2 * rem > TILE or 2 * radius > rows:
        raise NotImplementedError("radius")
    halo = 2 * full + (TILE if rem else 0)
    edge = full + (TILE if rem else 0)
    return full, rem, halo, edge


def kernel(
    n, bands, norm, radius, lev_width,
    g_hbm, p_hbm, w_hbm, lon_hbm, lat_hbm, lev_hbm, order_hbm,
    u_ref, out_ref,
    g_all, p_ref, pf_ref, w_ref, wn_ref, wh_ref, x_ref, z_ref, zn_ref, acc_ref, f_hi, f_lo, inc_ref, rs_ref,
    a_hi, a_lo, b_hi, b_lo, k_own, k_halo, k_fwd,
    lon_t, lat_t, lev_t, order,
    pool, known_sem, gr, zr, wr, rsr,
):
    me = lax.axis_index("mem")
    band = lax.axis_index("lat")
    members, _, levels, rows, lons = p_ref.shape
    own_levels = g_hbm.shape[1]
    width = 2 * radius + 1
    full, rem, halo, edge = sizes(rows, radius)
    stack = members * rows
    has_low, has_high = band > 0, band < bands - 1
    mesh_ids = pl.DeviceIdType.MESH

    free = list(range(pool.shape[0]))
    loads = [
        pltpu.make_async_copy(src, dst, pool.at[free.pop(0)])
        for i, (src, dst) in enumerate([
            (g_hbm, g_all.at[0]), (lon_hbm, lon_t), (order_hbm, order), (w_hbm, w_ref),
            (p_hbm, p_ref), (lev_hbm, lev_t), (lat_hbm, lat_t),
        ])
    ]
    g_in, lon_in, order_in, w_in, p_in, lev_in, lat_in = range(len(loads))
    for copy in loads:
        copy.start()

    barrier = pltpu.get_barrier_semaphore()
    cube = not n & (n - 1)
    direct = [d for d in range(1, n) if not cube or not d & (d - 1)]
    rounds = [[d for d in range(1, n) if not cube or bin(d).count("1") == hops]
              for hops in range(1, len(direct) + 1 if cube else 2)]
    arrival = [0] + [d for ds in rounds for d in ds]

    def greet(semaphore):
        for d in direct:
            pl.semaphore_signal(
                semaphore, inc=1, device_id=(partner(me, d, n), band), device_id_type=mesh_ids
            )

    greet(barrier)

    @pl.when(has_low)
    def _():
        pl.semaphore_signal(barrier, inc=1, device_id=(me, band - 1), device_id_type=mesh_ids)

    @pl.when(has_high)
    def _():
        pl.semaphore_signal(barrier, inc=1, device_id=(me, band + 1), device_id_type=mesh_ids)

    def source(d):
        return partner(me, d, n) if cube else (me + n - d) % n

    sent = []

    def remote(src, dst, recv_sem, sem, target):
        return pltpu.make_async_remote_copy(
            src_ref=src,
            dst_ref=dst,
            send_sem=pool.at[sem],
            recv_sem=recv_sem,
            device_id=target,
            device_id_type=mesh_ids,
        )

    def gather(d):
        sem = free.pop(0)
        copy = remote(g_all.at[0], g_all.at[d], gr.at[d - 1], sem, (partner(me, d, n), band))
        copy.start()
        sent.append((sem, copy.wait_send))
        return copy

    odd = band % 2
    far_then_near = ((1 - odd, band - 1 + 2 * odd, True), (odd, band + 1 - 2 * odd, True))
    both = has_low & has_high
    one = has_low ^ has_high

    def to_bands(pairs, piece, whole, recv_sem):
        sem = free.pop(0)
        for side, target, here in pairs:
            @pl.when((target >= 0) & (target < bands) & here)
            def _():
                remote(*piece(side), recv_sem, sem, (me, target)).start()

        def wait(semaphore):
            for count, here in ((2, both), (1, one)):
                ref = whole(count)
                pl.when(here)(pltpu.make_async_copy(ref, ref, semaphore).wait)

        sent.append((sem, lambda: wait(pool.at[sem])))
        return lambda: wait(recv_sem)

    def send_weights(size, low, high, recv_sem):
        at = ((low, low - rows + edge), (high, high))
        return to_bands(
            ((1, band - 1, odd == 0), (0, band + 1, True), (1, band - 1, odd == 1)),
            lambda side: (
                w_ref.at[:, :, at[side][0]:at[side][0] + size, :],
                wn_ref.at[side, :, :, at[side][1]:at[side][1] + size, :],
            ),
            lambda count: wn_ref.at[0:count, :, :, 0:size, :],
            recv_sem,
        )

    def settle(keep=0):
        for sem, wait in sent[:len(sent) - keep]:
            wait()
            free.append(sem)
        del sent[:len(sent) - keep]

    def loaded(i):
        loads[i].wait()
        free.append(i)

    loaded(g_in)
    loaded(lon_in)
    loaded(order_in)
    neighbours = has_low.astype(jnp.int32) + has_high.astype(jnp.int32)
    pl.semaphore_wait(barrier, len(direct) + neighbours)
    if len(rounds) > 1:
        greet(known_sem.at[0])
    gathers = {d: gather(d) for d in rounds[0]}
    loaded(w_in)
    w_arrival = [send_weights(full, rows - full, 0, wr.at[0])]
    if rem:
        w_arrival.append(send_weights(rem, rows - radius, full, wr.at[1]))

    row, col = iota((TILE, lons), 0), iota((TILE, lons), 1)

    def lon_matrix(c_hi, c_lo, sign):
        off = sign * (col - row) + radius
        off = jnp.where(off < 0, off + lons, off)
        off = jnp.where(off >= lons, off - lons, off)
        base = jnp.zeros((TILE, lons), F32)
        for j in range(width):
            base = jnp.where(off == j, lon_t[j], base)
        for i in range(0, lons, PACK):
            value = jnp.concatenate(
                [pltpu.roll(base, i, 1) if i else base, pltpu.roll(base, i + TILE, 1)], axis=0
            )
            c_hi[i:i + PACK], c_lo[i:i + PACK] = split(value)

    lon_matrix(a_hi, a_lo, 1)
    level_of = [
        order[source(q // own_levels) * own_levels + q % own_levels] for q in range(levels)
    ]
    loaded(p_in)

    def scaled(q):
        for v in range(2):
            for k in range(members):
                pf_ref[q, v, k * rows:(k + 1) * rows] = p_ref[k, v, level_of[q]].astype(F32) * norm

    z_arrival = {}
    ordered = [d * own_levels + j for d in arrival for j in range(own_levels)]
    parts = math.gcd(PARTS, members)
    unfiltered = ordered[own_levels:min(2 * own_levels, levels - 1)]

    def send_level(q):
        d, j = divmod(q, own_levels)
        g0 = jnp.concatenate([g_all[d, 0, j]] * members, axis=0)
        g1 = jnp.concatenate([g_all[d, 1, j]] * members, axis=0)
        x = pf_ref[q, 0] * g0 + pf_ref[q, 1] * g1
        src = z_ref.at[q]
        if q in unfiltered:
            src = x_ref.at[j]
            x_ref[j] = x
        else:
            z_ref[q] = filter_lon(x, a_hi, a_lo)
        size = stack // parts if q == ordered[-1] else stack
        z_arrival[q] = [
            to_bands(
                far_then_near,
                lambda side, at=at: (src.at[at:at + size], zn_ref.at[side, q, at:at + size]),
                lambda count, at=at: zn_ref.at[0:count, q, at:at + size],
                zr.at[levels + i - 1 if i else q],
            )
            for i, at in enumerate(range(0, stack, size))
        ]
        if q in unfiltered:
            z_ref[q] = filter_lon(x, a_hi, a_lo)

    early = len(sent)
    for j in range(own_levels):
        scaled(j)
        send_level(j)
    loaded(lev_in)
    loaded(lat_in)
    for i in range(1, len(rounds)):
        pl.semaphore_wait(known_sem.at[i - 1], len(direct))
        if i + 1 < len(rounds):
            greet(known_sem.at[i])
        gathers.update({d: gather(d) for d in rounds[i]})

    for q in range(own_levels, levels):
        scaled(q)
    for side, present in ((0, has_low), (1, has_high)):
        @pl.when(jnp.logical_not(present))
        def _():
            for q in range(levels):
                zn_ref[side, q] = jnp.zeros((stack, lons), F32)
            wn_ref[side] = jnp.zeros(wn_ref.shape[1:], F32)

    lon_matrix(b_hi, b_lo, -1)

    def thirds(shape):
        c, size = iota(shape, 1), shape[1] // 3
        third = (c >= size).astype(jnp.int32) + (c >= 2 * size).astype(jnp.int32)
        return third, c - third * size

    def halo_pos(h):
        s = h - 2 * full
        rest = jnp.where(s < rem, rows + full + s, s - full - TILE)
        rest = jnp.where((s >= rem) & (s < TILE - rem), -4 * rows, rest)
        return jnp.where(h < full, h - full, jnp.where(h < 2 * full, rows + h - full, rest))

    def lat_matrix(out_pos, in_pos, third, sign):
        shift = sign * (in_pos - out_pos)
        value = jnp.zeros(shift.shape, F32)
        for j in range(width):
            value = jnp.where(shift == j - radius, lat_t[j], value)
        high = value.astype(BF16).astype(F32)
        return jnp.where(third == 1, value - high, high).astype(BF16)

    far = 8 * rows
    for k_ref, is_own in ((k_own, True), (k_halo, False)):
        r = iota(k_ref.shape, 0)
        third, c = thirds(k_ref.shape)
        if is_own:
            in_pos = jnp.where(c < rows, c, far)
        else:
            in_pos = jnp.where(c < rows, c - rows, jnp.where(c < 2 * rows, c, far))
        out_pos = jnp.where(r < rows, r, halo_pos(r - rows))
        k_ref[...] = lat_matrix(out_pos, in_pos, third, -1)
    third, c = thirds(k_fwd.shape)
    in_pos = jnp.where(c < rows, c, halo_pos(c - rows))
    inside = (in_pos + band * rows >= 0) & (in_pos + band * rows < bands * rows)
    inside = inside & (c < rows + halo)
    k_fwd[...] = lat_matrix(iota(k_fwd.shape, 0), jnp.where(inside, in_pos, far), third, 1)

    coef = []
    for l in range(levels):
        coef.append([])
        for q in range(levels):
            tap = l - level_of[q] + lev_width // 2
            inside = (tap >= 0) & (tap < lev_width)
            value = lev_t[jnp.clip(tap, 0, lev_width - 1)]
            coef[l].append(jnp.where(inside, value, 0.0))

    for d in arrival[1:]:
        if d == arrival[2]:
            settle(keep=len(sent) - early)
        gathers[d].wait_recv()
        for j in range(own_levels):
            send_level(d * own_levels + j)

    for wait in w_arrival:
        wait()
    s = iota((TILE, lons), 0)
    for k in range(members):
        at = slice(k * rows, (k + 1) * rows)
        for l in range(levels):
            wh_ref[k, l, 0:full] = wn_ref[0, k, l, edge - full:edge]
            wh_ref[k, l, full:2 * full] = wn_ref[1, k, l, 0:full]
            if rem:
                wh_ref[k, l, 2 * full:halo] = jnp.where(
                    s < rem, wn_ref[1, k, l, full:edge], wn_ref[0, k, l, 0:TILE]
                )
        own = [dot(k_own[...], stacked(z_ref[q, at])) for q in range(levels)]
        for l in range(levels):
            total = jnp.concatenate([w_ref[k, l], wh_ref[k, l]], axis=0)
            for q in range(levels):
                total = total + coef[l][q] * own[q]
            acc_ref[k, l] = total

    for q in ordered[:-1]:
        z_arrival[q][0]()
        if q in unfiltered:
            z = filter_lon(jnp.concatenate([zn_ref[0, q], zn_ref[1, q]], axis=0), a_hi, a_lo)
            zn_ref[0, q], zn_ref[1, q] = z[:stack], z[stack:]
        for k in range(members):
            at = slice(k * rows, (k + 1) * rows)
            y = dot(k_halo[...], stacked(jnp.concatenate([zn_ref[0, q, at], zn_ref[1, q, at]], axis=0)))
            for l in range(levels):
                acc_ref[k, l] = acc_ref[k, l] + coef[l][q] * y

    settle(keep=parts)
    q = ordered[-1]
    backward = arrival[::-1]
    outgoing = [d * own_levels + j for d in backward[:-1] for j in range(own_levels)]
    part = stack // parts

    def filtered_part(g):
        at = slice(g * part, (g + 1) * part)
        high = jnp.concatenate([f_hi[j, at] for j in outgoing], axis=0)
        low = jnp.concatenate([f_lo[j, at] for j in outgoing], axis=0)
        return filter_split(high, low, b_hi, b_lo)

    for i in range(parts):
        z_arrival[q][i]()
        group = range(i * members // parts, (i + 1) * members // parts)
        last = {}
        for k in group:
            at = slice(k * rows, (k + 1) * rows)
            x = jnp.concatenate([zn_ref[0, q, at], zn_ref[1, q, at]], axis=0)
            last[k] = dot(k_halo[...], stacked(x))
        if i == parts - 1:
            filtered = [filtered_part(g) for g in range(i)]
        fields = {j: [] for j in range(levels)}
        for k in group:
            y = []
            for l in range(levels):
                w = jnp.concatenate([w_ref[k, l], wh_ref[k, l]], axis=0)
                total = acc_ref[k, l] + coef[l][q] * last[k]
                u = w - STEP_RATE * total / (1.0 + jnp.abs(total))
                u_ref[k, l] = u[0:rows]
                y.append(dot(k_fwd[...], stacked(u)))
            for j in range(levels):
                field = coef[0][j] * y[0]
                for l in range(1, levels):
                    field = field + coef[l][j] * y[l]
                fields[j].append(field)
        at = slice(group[0] * rows, (group[-1] + 1) * rows)
        for j in range(levels):
            f_hi[j, at], f_lo[j, at] = split(jnp.concatenate(fields[j], axis=0))

    scatter_sem = free.pop(0)
    filtered.append(filtered_part(parts - 1))

    def increment(q, fields):
        for v in range(2):
            inc = None
            for g, field in enumerate(fields):
                terms = pf_ref[q, v, g * field.shape[0]:(g + 1) * field.shape[0]] * field
                for k in range(0, field.shape[0], rows):
                    term = terms[k:k + rows]
                    inc = term if inc is None else inc + term
            inc_ref[q // own_levels, v, q % own_levels] = inc

    for i, q in enumerate(outgoing):
        increment(q, [f[i * part:(i + 1) * part] for f in filtered])
        d = q // own_levels
        if (q + 1) % own_levels == 0:
            remote(inc_ref.at[d], rs_ref.at[d - 1], rsr, scatter_sem, (source(d), band)).start()
    for q in range(own_levels):
        increment(q, [filter_split(f_hi[q], f_lo[q], b_hi, b_lo)])
    settle()
    pltpu.make_async_copy(rs_ref, rs_ref, rsr).wait()
    result = inc_ref[0]
    for d in range(1, n):
        result = result + rs_ref[d - 1]
    out_ref[...] = result
    pltpu.make_async_copy(rs_ref, rs_ref, pool.at[scatter_sem]).wait()


def write_out(u_ref, inc_ref, upd_hbm, inc_hbm, sem):
    first = pltpu.make_async_copy(u_ref, upd_hbm, sem.at[0])
    second = pltpu.make_async_copy(inc_ref, inc_hbm, sem.at[1])
    first.start()
    second.start()
    first.wait()
    second.wait()


def on_device(gradient, perturbations, weights, lon_taps, lat_taps, lev_taps, level_order):
    n, bands = lax.axis_size("mem"), lax.axis_size("lat")
    members, levels, rows, lons = weights.shape
    radius = lat_taps.shape[0] // 2
    norm = 1.0 / math.sqrt(members * n - 1)
    full, rem, halo, edge = sizes(rows, radius)
    stack = members * rows
    vmem, dma = pltpu.VMEM, pltpu.SemaphoreType.DMA
    anywhere = pl.BlockSpec(memory_space=pl.ANY)
    in_vmem = pl.BlockSpec(memory_space=pltpu.VMEM)
    updated, increment = pl.pallas_call(
        functools.partial(kernel, n, bands, norm, radius, lev_taps.shape[0]),
        out_shape=(
            vmem(weights.shape, F32),
            vmem(gradient.shape, F32),
        ),
        in_specs=[anywhere] * 7,
        out_specs=(in_vmem, in_vmem),
        scratch_shapes=[
            vmem((n,) + gradient.shape, F32),
            vmem(perturbations.shape, BF16),
            vmem((levels, 2, stack, lons), F32),
            vmem(weights.shape, F32),
            vmem((2, members, levels, edge, lons), F32),
            vmem((members, levels, halo, lons), F32),
            vmem((gradient.shape[1], stack, lons), F32),
            vmem((levels, stack, lons), F32),
            vmem((2, levels, stack, lons), F32),
            vmem((members, levels, rows + halo, lons), F32),
            vmem((levels, stack, lons), BF16),
            vmem((levels, stack, lons), BF16),
            vmem((n,) + gradient.shape, F32),
            vmem((n - 1,) + gradient.shape, F32),
            vmem((lons, lons), BF16),
            vmem((lons, lons), BF16),
            vmem((lons, lons), BF16),
            vmem((lons, lons), BF16),
            vmem((rows + halo, 3 * packed(rows)), BF16),
            vmem((rows + halo, 3 * packed(2 * rows)), BF16),
            vmem((rows, 3 * packed(rows + halo)), BF16),
            pltpu.SMEM(lon_taps.shape, F32),
            pltpu.SMEM(lat_taps.shape, F32),
            pltpu.SMEM(lev_taps.shape, F32),
            pltpu.SMEM(level_order.shape, jnp.int32),
            dma((max(7, n + levels - 1),)),
            pltpu.SemaphoreType.REGULAR((max(1, n.bit_length() - 2),)),
            dma((n - 1,)),
            dma((levels + math.gcd(PARTS, members) - 1,)),
            dma((2,)),
            dma,
        ],
        compiler_params=pltpu.CompilerParams(collective_id=0, has_side_effects=True),
        name="step",
    )(gradient, perturbations, weights, lon_taps, lat_taps, lev_taps, level_order)
    return pl.pallas_call(
        write_out,
        out_shape=(
            jax.ShapeDtypeStruct(updated.shape, F32),
            jax.ShapeDtypeStruct(increment.shape, F32),
        ),
        in_specs=[in_vmem] * 2,
        out_specs=(anywhere, anywhere),
        scratch_shapes=[dma((2,))],
        name="write_out",
    )(
        pltpu.with_memory_space_constraint(updated, pltpu.VMEM),
        pltpu.with_memory_space_constraint(increment, pltpu.VMEM),
    )


def solution(mesh):
    in_specs = (
        P(None, "mem", "lat", None),
        P("mem", None, None, "lat", None),
        P("mem", None, "lat", None),
        P(),
        P(),
        P(),
        P(),
    )
    out_specs = (P("mem", None, "lat", None), P(None, "mem", "lat", None))
    return jax.shard_map(
        on_device, mesh=mesh, in_specs=in_specs, out_specs=out_specs, check_vma=False
    )
```

```python
import functools
import math

import jax
import jax.numpy as jnp
from jax import lax
from jax.experimental import pallas as pl
from jax.experimental.pallas import tpu as pltpu
from jax.sharding import PartitionSpec as P

STEP_RATE = 0.5
TILE = 8
PACK = 16
PARTS = 2
F32 = jnp.float32
BF16 = jnp.bfloat16


def partner(me, d, n):
    if n & (n - 1):
        return (me + d) % n
    result = 0
    bit = 1
    while bit < n:
        result = result + ((me // bit + d // bit) % 2) * bit
        bit *= 2
    return result


def split(x):
    high = x.astype(BF16)
    return high, (x - high.astype(F32)).astype(BF16)


def dot(a, b):
    return lax.dot_general(a, b, (((1,), (0,)), ((), ())), preferred_element_type=F32)


def filter_split(high, low, c_hi, c_lo):
    size = high.shape[0]
    both = dot(jnp.concatenate([high, low], axis=0), c_hi[...])
    return both[:size] + (both[size:] + dot(high, c_lo[...]))


def filter_lon(x, c_hi, c_lo):
    return filter_split(*split(x), c_hi, c_lo)


def packed(rows):
    return -(-rows // PACK) * PACK


def stacked(x):
    pad = packed(x.shape[0]) - x.shape[0]
    if pad:
        x = jnp.concatenate([x, jnp.zeros((pad, x.shape[1]), F32)], axis=0)
    high, low = split(x)
    return jnp.concatenate([high, high, low], axis=0)


def iota(shape, axis):
    return lax.broadcasted_iota(jnp.int32, shape, axis)


def sizes(rows, radius):
    full = radius // TILE * TILE
    rem = radius - full
    if 2 * rem > TILE or 2 * radius > rows:
        raise NotImplementedError("radius")
    halo = 2 * full + (TILE if rem else 0)
    edge = full + (TILE if rem else 0)
    return full, rem, halo, edge


def kernel(
    n, bands, norm, radius, lev_width,
    g_hbm, p_hbm, w_hbm, lon_hbm, lat_hbm, lev_hbm, order_hbm,
    u_ref, out_ref,
    g_all, p_ref, pf_ref, w_ref, wn_ref, wh_ref, x_ref, z_ref, zn_ref, acc_ref, f_hi, f_lo, inc_ref, rs_ref,
    a_hi, a_lo, b_hi, b_lo, k_own, k_halo, k_fwd,
    lon_t, lat_t, lev_t, order,
    pool, known_sem, gr, zr, wr, rsr,
):
    me = lax.axis_index("mem")
    band = lax.axis_index("lat")
    members, _, levels, rows, lons = p_ref.shape
    own_levels = g_hbm.shape[1]
    width = 2 * radius + 1
    full, rem, halo, edge = sizes(rows, radius)
    stack = members * rows
    has_low, has_high = band > 0, band < bands - 1
    mesh_ids = pl.DeviceIdType.MESH

    free = list(range(pool.shape[0]))
    loads = [
        pltpu.make_async_copy(src, dst, pool.at[free.pop(0)])
        for i, (src, dst) in enumerate([
            (g_hbm, g_all.at[0]), (lon_hbm, lon_t), (order_hbm, order), (w_hbm, w_ref),
            (p_hbm, p_ref), (lev_hbm, lev_t), (lat_hbm, lat_t),
        ])
    ]
    g_in, lon_in, order_in, w_in, p_in, lev_in, lat_in = range(len(loads))
    loads[g_in].start()

    barrier = pltpu.get_barrier_semaphore()
    cube = not n & (n - 1)
    direct = [d for d in range(1, n) if not cube or not d & (d - 1)]
    rounds = [[d for d in range(1, n) if not cube or bin(d).count("1") == hops]
              for hops in range(1, len(direct) + 1 if cube else 2)]
    arrival = [0] + [d for ds in rounds for d in ds]

    def greet(semaphore):
        for d in direct:
            pl.semaphore_signal(
                semaphore, inc=1, device_id=(partner(me, d, n), band), device_id_type=mesh_ids
            )

    greet(barrier)

    @pl.when(has_low)
    def _():
        pl.semaphore_signal(barrier, inc=1, device_id=(me, band - 1), device_id_type=mesh_ids)

    @pl.when(has_high)
    def _():
        pl.semaphore_signal(barrier, inc=1, device_id=(me, band + 1), device_id_type=mesh_ids)

    for copy in loads[1:]:
        copy.start()

    def source(d):
        return partner(me, d, n) if cube else (me + n - d) % n

    sent = []

    def remote(src, dst, recv_sem, sem, target):
        return pltpu.make_async_remote_copy(
            src_ref=src,
            dst_ref=dst,
            send_sem=pool.at[sem],
            recv_sem=recv_sem,
            device_id=target,
            device_id_type=mesh_ids,
        )

    def gather(d):
        sem = free.pop(0)
        copy = remote(g_all.at[0], g_all.at[d], gr.at[d - 1], sem, (partner(me, d, n), band))
        copy.start()
        sent.append((sem, copy.wait_send))
        return copy

    odd = band % 2
    far_then_near = ((1 - odd, band - 1 + 2 * odd, True), (odd, band + 1 - 2 * odd, True))
    both = has_low & has_high
    one = has_low ^ has_high

    def to_bands(pairs, piece, whole, recv_sem):
        sem = free.pop(0)
        for side, target, here in pairs:
            @pl.when((target >= 0) & (target < bands) & here)
            def _():
                remote(*piece(side), recv_sem, sem, (me, target)).start()

        def wait(semaphore):
            for count, here in ((2, both), (1, one)):
                ref = whole(count)
                pl.when(here)(pltpu.make_async_copy(ref, ref, semaphore).wait)

        sent.append((sem, lambda: wait(pool.at[sem])))
        return lambda: wait(recv_sem)

    def send_weights(size, low, high, recv_sem):
        at = ((low, low - rows + edge), (high, high))
        return to_bands(
            ((1, band - 1, odd == 0), (0, band + 1, True), (1, band - 1, odd == 1)),
            lambda side: (
                w_ref.at[:, :, at[side][0]:at[side][0] + size, :],
                wn_ref.at[side, :, :, at[side][1]:at[side][1] + size, :],
            ),
            lambda count: wn_ref.at[0:count, :, :, 0:size, :],
            recv_sem,
        )

    def settle(keep=0):
        for sem, wait in sent[:len(sent) - keep]:
            wait()
            free.append(sem)
        del sent[:len(sent) - keep]

    def loaded(i):
        loads[i].wait()
        free.append(i)

    loaded(g_in)
    loaded(lon_in)
    loaded(order_in)
    neighbours = has_low.astype(jnp.int32) + has_high.astype(jnp.int32)
    pl.semaphore_wait(barrier, len(direct) + neighbours)
    if len(rounds) > 1:
        greet(known_sem.at[0])
    gathers = {d: gather(d) for d in rounds[0]}
    loaded(w_in)
    w_arrival = [send_weights(full, rows - full, 0, wr.at[0])]
    if rem:
        w_arrival.append(send_weights(rem, rows - radius, full, wr.at[1]))

    row, col = iota((TILE, lons), 0), iota((TILE, lons), 1)

    def lon_matrix(c_hi, c_lo, sign):
        off = sign * (col - row) + radius
        off = jnp.where(off < 0, off + lons, off)
        off = jnp.where(off >= lons, off - lons, off)
        base = jnp.zeros((TILE, lons), F32)
        for j in range(width):
            base = jnp.where(off == j, lon_t[j], base)
        for i in range(0, lons, PACK):
            value = jnp.concatenate(
                [pltpu.roll(base, i, 1) if i else base, pltpu.roll(base, i + TILE, 1)], axis=0
            )
            c_hi[i:i + PACK], c_lo[i:i + PACK] = split(value)

    lon_matrix(a_hi, a_lo, 1)
    level_of = [
        order[source(q // own_levels) * own_levels + q % own_levels] for q in range(levels)
    ]
    loaded(p_in)

    def scaled(q):
        for v in range(2):
            for k in range(members):
                pf_ref[q, v, k * rows:(k + 1) * rows] = p_ref[k, v, level_of[q]].astype(F32) * norm

    z_arrival = {}
    ordered = [d * own_levels + j for d in arrival for j in range(own_levels)]
    parts = math.gcd(PARTS, members)
    unfiltered = ordered[own_levels:min(2 * own_levels, levels - 1)]

    def send_level(q):
        d, j = divmod(q, own_levels)
        g0 = jnp.concatenate([g_all[d, 0, j]] * members, axis=0)
        g1 = jnp.concatenate([g_all[d, 1, j]] * members, axis=0)
        x = pf_ref[q, 0] * g0 + pf_ref[q, 1] * g1
        src = z_ref.at[q]
        if q in unfiltered:
            src = x_ref.at[j]
            x_ref[j] = x
        else:
            z_ref[q] = filter_lon(x, a_hi, a_lo)
        size = stack // parts if q == ordered[-1] else stack
        z_arrival[q] = [
            to_bands(
                far_then_near,
                lambda side, at=at: (src.at[at:at + size], zn_ref.at[side, q, at:at + size]),
                lambda count, at=at: zn_ref.at[0:count, q, at:at + size],
                zr.at[levels + i - 1 if i else q],
            )
            for i, at in enumerate(range(0, stack, size))
        ]
        if q in unfiltered:
            z_ref[q] = filter_lon(x, a_hi, a_lo)

    early = len(sent)
    for j in range(own_levels):
        scaled(j)
        send_level(j)
    loaded(lev_in)
    loaded(lat_in)
    for i in range(1, len(rounds)):
        pl.semaphore_wait(known_sem.at[i - 1], len(direct))
        if i + 1 < len(rounds):
            greet(known_sem.at[i])
        gathers.update({d: gather(d) for d in rounds[i]})

    for q in range(own_levels, levels):
        scaled(q)
    for side, present in ((0, has_low), (1, has_high)):
        @pl.when(jnp.logical_not(present))
        def _():
            for q in range(levels):
                zn_ref[side, q] = jnp.zeros((stack, lons), F32)
            wn_ref[side] = jnp.zeros(wn_ref.shape[1:], F32)

    lon_matrix(b_hi, b_lo, -1)

    def thirds(shape):
        c, size = iota(shape, 1), shape[1] // 3
        third = (c >= size).astype(jnp.int32) + (c >= 2 * size).astype(jnp.int32)
        return third, c - third * size

    def halo_pos(h):
        s = h - 2 * full
        rest = jnp.where(s < rem, rows + full + s, s - full - TILE)
        rest = jnp.where((s >= rem) & (s < TILE - rem), -4 * rows, rest)
        return jnp.where(h < full, h - full, jnp.where(h < 2 * full, rows + h - full, rest))

    def lat_matrix(out_pos, in_pos, third, sign):
        shift = sign * (in_pos - out_pos)
        value = jnp.zeros(shift.shape, F32)
        for j in range(width):
            value = jnp.where(shift == j - radius, lat_t[j], value)
        high = value.astype(BF16).astype(F32)
        return jnp.where(third == 1, value - high, high).astype(BF16)

    far = 8 * rows
    for k_ref, is_own in ((k_own, True), (k_halo, False)):
        r = iota(k_ref.shape, 0)
        third, c = thirds(k_ref.shape)
        if is_own:
            in_pos = jnp.where(c < rows, c, far)
        else:
            in_pos = jnp.where(c < rows, c - rows, jnp.where(c < 2 * rows, c, far))
        out_pos = jnp.where(r < rows, r, halo_pos(r - rows))
        k_ref[...] = lat_matrix(out_pos, in_pos, third, -1)
    third, c = thirds(k_fwd.shape)
    in_pos = jnp.where(c < rows, c, halo_pos(c - rows))
    inside = (in_pos + band * rows >= 0) & (in_pos + band * rows < bands * rows)
    inside = inside & (c < rows + halo)
    k_fwd[...] = lat_matrix(iota(k_fwd.shape, 0), jnp.where(inside, in_pos, far), third, 1)

    coef = []
    for l in range(levels):
        coef.append([])
        for q in range(levels):
            tap = l - level_of[q] + lev_width // 2
            inside = (tap >= 0) & (tap < lev_width)
            value = lev_t[jnp.clip(tap, 0, lev_width - 1)]
            coef[l].append(jnp.where(inside, value, 0.0))

    for d in arrival[1:]:
        if d == arrival[2]:
            settle(keep=len(sent) - early)
        gathers[d].wait_recv()
        for j in range(own_levels):
            send_level(d * own_levels + j)

    for wait in w_arrival:
        wait()
    s = iota((TILE, lons), 0)
    for k in range(members):
        at = slice(k * rows, (k + 1) * rows)
        for l in range(levels):
            wh_ref[k, l, 0:full] = wn_ref[0, k, l, edge - full:edge]
            wh_ref[k, l, full:2 * full] = wn_ref[1, k, l, 0:full]
            if rem:
                wh_ref[k, l, 2 * full:halo] = jnp.where(
                    s < rem, wn_ref[1, k, l, full:edge], wn_ref[0, k, l, 0:TILE]
                )
        own = [dot(k_own[...], stacked(z_ref[q, at])) for q in range(levels)]
        for l in range(levels):
            total = jnp.concatenate([w_ref[k, l], wh_ref[k, l]], axis=0)
            for q in range(levels):
                total = total + coef[l][q] * own[q]
            acc_ref[k, l] = total

    for q in ordered[:-1]:
        z_arrival[q][0]()
        if q in unfiltered:
            z = filter_lon(jnp.concatenate([zn_ref[0, q], zn_ref[1, q]], axis=0), a_hi, a_lo)
            zn_ref[0, q], zn_ref[1, q] = z[:stack], z[stack:]
        for k in range(members):
            at = slice(k * rows, (k + 1) * rows)
            y = dot(k_halo[...], stacked(jnp.concatenate([zn_ref[0, q, at], zn_ref[1, q, at]], axis=0)))
            for l in range(levels):
                acc_ref[k, l] = acc_ref[k, l] + coef[l][q] * y

    settle(keep=parts)
    q = ordered[-1]
    backward = arrival[::-1]
    outgoing = [d * own_levels + j for d in backward[:-1] for j in range(own_levels)]
    part = stack // parts

    def filtered_part(g):
        at = slice(g * part, (g + 1) * part)
        high = jnp.concatenate([f_hi[j, at] for j in outgoing], axis=0)
        low = jnp.concatenate([f_lo[j, at] for j in outgoing], axis=0)
        return filter_split(high, low, b_hi, b_lo)

    for i in range(parts):
        z_arrival[q][i]()
        group = range(i * members // parts, (i + 1) * members // parts)
        last = {}
        for k in group:
            at = slice(k * rows, (k + 1) * rows)
            x = jnp.concatenate([zn_ref[0, q, at], zn_ref[1, q, at]], axis=0)
            last[k] = dot(k_halo[...], stacked(x))
        if i == parts - 1:
            filtered = [filtered_part(g) for g in range(i)]
        fields = {j: [] for j in range(levels)}
        for k in group:
            y = []
            for l in range(levels):
                w = jnp.concatenate([w_ref[k, l], wh_ref[k, l]], axis=0)
                total = acc_ref[k, l] + coef[l][q] * last[k]
                u = w - STEP_RATE * total / (1.0 + jnp.abs(total))
                u_ref[k, l] = u[0:rows]
                y.append(dot(k_fwd[...], stacked(u)))
            for j in range(levels):
                field = coef[0][j] * y[0]
                for l in range(1, levels):
                    field = field + coef[l][j] * y[l]
                fields[j].append(field)
        at = slice(group[0] * rows, (group[-1] + 1) * rows)
        for j in range(levels):
            f_hi[j, at], f_lo[j, at] = split(jnp.concatenate(fields[j], axis=0))

    scatter_sem = free.pop(0)
    filtered.append(filtered_part(parts - 1))

    def increment(q, fields):
        for v in range(2):
            inc = None
            for g, field in enumerate(fields):
                terms = pf_ref[q, v, g * field.shape[0]:(g + 1) * field.shape[0]] * field
                for k in range(0, field.shape[0], rows):
                    term = terms[k:k + rows]
                    inc = term if inc is None else inc + term
            inc_ref[q // own_levels, v, q % own_levels] = inc

    for i, q in enumerate(outgoing):
        increment(q, [f[i * part:(i + 1) * part] for f in filtered])
        d = q // own_levels
        if (q + 1) % own_levels == 0:
            remote(inc_ref.at[d], rs_ref.at[d - 1], rsr, scatter_sem, (source(d), band)).start()
    for q in range(own_levels):
        increment(q, [filter_split(f_hi[q], f_lo[q], b_hi, b_lo)])
    settle()
    pltpu.make_async_copy(rs_ref, rs_ref, rsr).wait()
    result = inc_ref[0]
    for d in range(1, n):
        result = result + rs_ref[d - 1]
    out_ref[...] = result
    pltpu.make_async_copy(rs_ref, rs_ref, pool.at[scatter_sem]).wait()


def write_out(u_ref, inc_ref, upd_hbm, inc_hbm, sem):
    first = pltpu.make_async_copy(u_ref, upd_hbm, sem.at[0])
    second = pltpu.make_async_copy(inc_ref, inc_hbm, sem.at[1])
    first.start()
    second.start()
    first.wait()
    second.wait()


def on_device(gradient, perturbations, weights, lon_taps, lat_taps, lev_taps, level_order):
    n, bands = lax.axis_size("mem"), lax.axis_size("lat")
    members, levels, rows, lons = weights.shape
    radius = lat_taps.shape[0] // 2
    norm = 1.0 / math.sqrt(members * n - 1)
    full, rem, halo, edge = sizes(rows, radius)
    stack = members * rows
    vmem, dma = pltpu.VMEM, pltpu.SemaphoreType.DMA
    anywhere = pl.BlockSpec(memory_space=pl.ANY)
    in_vmem = pl.BlockSpec(memory_space=pltpu.VMEM)
    updated, increment = pl.pallas_call(
        functools.partial(kernel, n, bands, norm, radius, lev_taps.shape[0]),
        out_shape=(
            vmem(weights.shape, F32),
            vmem(gradient.shape, F32),
        ),
        in_specs=[anywhere] * 7,
        out_specs=(in_vmem, in_vmem),
        scratch_shapes=[
            vmem((n,) + gradient.shape, F32),
            vmem(perturbations.shape, BF16),
            vmem((levels, 2, stack, lons), F32),
            vmem(weights.shape, F32),
            vmem((2, members, levels, edge, lons), F32),
            vmem((members, levels, halo, lons), F32),
            vmem((gradient.shape[1], stack, lons), F32),
            vmem((levels, stack, lons), F32),
            vmem((2, levels, stack, lons), F32),
            vmem((members, levels, rows + halo, lons), F32),
            vmem((levels, stack, lons), BF16),
            vmem((levels, stack, lons), BF16),
            vmem((n,) + gradient.shape, F32),
            vmem((n - 1,) + gradient.shape, F32),
            vmem((lons, lons), BF16),
            vmem((lons, lons), BF16),
            vmem((lons, lons), BF16),
            vmem((lons, lons), BF16),
            vmem((rows + halo, 3 * packed(rows)), BF16),
            vmem((rows + halo, 3 * packed(2 * rows)), BF16),
            vmem((rows, 3 * packed(rows + halo)), BF16),
            pltpu.SMEM(lon_taps.shape, F32),
            pltpu.SMEM(lat_taps.shape, F32),
            pltpu.SMEM(lev_taps.shape, F32),
            pltpu.SMEM(level_order.shape, jnp.int32),
            dma((max(7, n + levels - 1),)),
            pltpu.SemaphoreType.REGULAR((max(1, n.bit_length() - 2),)),
            dma((n - 1,)),
            dma((levels + math.gcd(PARTS, members) - 1,)),
            dma((2,)),
            dma,
        ],
        compiler_params=pltpu.CompilerParams(collective_id=0, has_side_effects=True),
        name="step",
    )(gradient, perturbations, weights, lon_taps, lat_taps, lev_taps, level_order)
    return pl.pallas_call(
        write_out,
        out_shape=(
            jax.ShapeDtypeStruct(updated.shape, F32),
            jax.ShapeDtypeStruct(increment.shape, F32),
        ),
        in_specs=[in_vmem] * 2,
        out_specs=(anywhere, anywhere),
        scratch_shapes=[dma((2,))],
        name="write_out",
    )(
        pltpu.with_memory_space_constraint(updated, pltpu.VMEM),
        pltpu.with_memory_space_constraint(increment, pltpu.VMEM),
    )


def solution(mesh):
    in_specs = (
        P(None, "mem", "lat", None),
        P("mem", None, None, "lat", None),
        P("mem", None, "lat", None),
        P(),
        P(),
        P(),
        P(),
    )
    out_specs = (P("mem", None, "lat", None), P(None, "mem", "lat", None))
    return jax.shard_map(
        on_device, mesh=mesh, in_specs=in_specs, out_specs=out_specs, check_vma=False
    )
```

```python
import functools
import math

import jax
import jax.numpy as jnp
from jax import lax
from jax.experimental import pallas as pl
from jax.experimental.pallas import tpu as pltpu
from jax.sharding import PartitionSpec as P

STEP_RATE = 0.5
TILE = 8
PACK = 16
PARTS = 2
F32 = jnp.float32
BF16 = jnp.bfloat16


def partner(me, d, n):
    if n & (n - 1):
        return (me + d) % n
    result = 0
    bit = 1
    while bit < n:
        result = result + ((me // bit + d // bit) % 2) * bit
        bit *= 2
    return result


def split(x):
    high = x.astype(BF16)
    return high, (x - high.astype(F32)).astype(BF16)


def dot(a, b):
    return lax.dot_general(a, b, (((1,), (0,)), ((), ())), preferred_element_type=F32)


def filter_split(high, low, c_hi, c_lo):
    size = high.shape[0]
    both = dot(jnp.concatenate([high, low], axis=0), c_hi[...])
    return both[:size] + (both[size:] + dot(high, c_lo[...]))


def filter_lon(x, c_hi, c_lo):
    return filter_split(*split(x), c_hi, c_lo)


def packed(rows):
    return -(-rows // PACK) * PACK


def stacked(x):
    pad = packed(x.shape[0]) - x.shape[0]
    if pad:
        x = jnp.concatenate([x, jnp.zeros((pad, x.shape[1]), F32)], axis=0)
    high, low = split(x)
    return jnp.concatenate([high, high, low], axis=0)


def iota(shape, axis):
    return lax.broadcasted_iota(jnp.int32, shape, axis)


def sizes(rows, radius):
    full = radius // TILE * TILE
    rem = radius - full
    if 2 * rem > TILE or 2 * radius > rows:
        raise NotImplementedError("radius")
    halo = 2 * full + (TILE if rem else 0)
    edge = full + (TILE if rem else 0)
    return full, rem, halo, edge


def kernel(
    n, bands, norm, radius, lev_width,
    g_hbm, p_hbm, w_hbm, lon_hbm, lat_hbm, lev_hbm, order_hbm,
    u_ref, out_ref,
    g_all, p_ref, pf_ref, w_ref, wn_ref, wh_ref, x_ref, z_ref, zn_ref, acc_ref, f_hi, f_lo, inc_ref, rs_ref,
    a_hi, a_lo, b_hi, b_lo, k_own, k_halo, k_fwd,
    lon_t, lat_t, lev_t, order,
    pool, known_sem, gr, zr, wr, rsr,
):
    me = lax.axis_index("mem")
    band = lax.axis_index("lat")
    members, _, levels, rows, lons = p_ref.shape
    own_levels = g_hbm.shape[1]
    width = 2 * radius + 1
    full, rem, halo, edge = sizes(rows, radius)
    stack = members * rows
    has_low, has_high = band > 0, band < bands - 1
    mesh_ids = pl.DeviceIdType.MESH

    free = list(range(pool.shape[0]))
    loads = [
        pltpu.make_async_copy(src, dst, pool.at[free.pop(0)])
        for i, (src, dst) in enumerate([
            (g_hbm, g_all.at[0]), (lon_hbm, lon_t), (order_hbm, order), (w_hbm, w_ref),
            (p_hbm, p_ref), (lev_hbm, lev_t), (lat_hbm, lat_t),
        ])
    ]
    g_in, lon_in, order_in, w_in, p_in, lev_in, lat_in = range(len(loads))
    for copy in loads:
        copy.start()

    barrier = pltpu.get_barrier_semaphore()
    cube = not n & (n - 1)
    direct = [d for d in range(1, n) if not cube or not d & (d - 1)]
    rounds = [[d for d in range(1, n) if not cube or bin(d).count("1") == hops]
              for hops in range(1, len(direct) + 1 if cube else 2)]
    arrival = [0] + [d for ds in rounds for d in ds]

    def greet(semaphore):
        for d in direct:
            pl.semaphore_signal(
                semaphore, inc=1, device_id=(partner(me, d, n), band), device_id_type=mesh_ids
            )

    greet(barrier)

    @pl.when(has_low)
    def _():
        pl.semaphore_signal(barrier, inc=1, device_id=(me, band - 1), device_id_type=mesh_ids)

    @pl.when(has_high)
    def _():
        pl.semaphore_signal(barrier, inc=1, device_id=(me, band + 1), device_id_type=mesh_ids)

    def source(d):
        return partner(me, d, n) if cube else (me + n - d) % n

    sent = []

    def remote(src, dst, recv_sem, sem, target):
        return pltpu.make_async_remote_copy(
            src_ref=src,
            dst_ref=dst,
            send_sem=pool.at[sem],
            recv_sem=recv_sem,
            device_id=target,
            device_id_type=mesh_ids,
        )

    def gather(d):
        sem = free.pop(0)
        copy = remote(g_all.at[0], g_all.at[d], gr.at[d - 1], sem, (partner(me, d, n), band))
        copy.start()
        sent.append((sem, copy.wait_send))
        return copy

    odd = band % 2
    far_then_near = ((1 - odd, band - 1 + 2 * odd, True), (odd, band + 1 - 2 * odd, True))
    both = has_low & has_high
    one = has_low ^ has_high

    def to_bands(pairs, piece, whole, recv_sem):
        sem = free.pop(0)
        for side, target, here in pairs:
            @pl.when((target >= 0) & (target < bands) & here)
            def _():
                remote(*piece(side), recv_sem, sem, (me, target)).start()

        def wait(semaphore):
            for count, here in ((2, both), (1, one)):
                ref = whole(count)
                pl.when(here)(pltpu.make_async_copy(ref, ref, semaphore).wait)

        sent.append((sem, lambda: wait(pool.at[sem])))
        return lambda: wait(recv_sem)

    def send_weights(size, low, high, recv_sem):
        at = ((low, low - rows + edge), (high, high))
        return to_bands(
            ((1, band - 1, odd == 0), (0, band + 1, True), (1, band - 1, odd == 1)),
            lambda side: (
                w_ref.at[:, :, at[side][0]:at[side][0] + size, :],
                wn_ref.at[side, :, :, at[side][1]:at[side][1] + size, :],
            ),
            lambda count: wn_ref.at[0:count, :, :, 0:size, :],
            recv_sem,
        )

    def settle(keep=0):
        for sem, wait in sent[:len(sent) - keep]:
            wait()
            free.append(sem)
        del sent[:len(sent) - keep]

    def loaded(i):
        loads[i].wait()
        free.append(i)

    loaded(g_in)
    loaded(lon_in)
    loaded(order_in)
    neighbours = has_low.astype(jnp.int32) + has_high.astype(jnp.int32)
    pl.semaphore_wait(barrier, len(direct) + neighbours)
    gathers = {d: gather(d) for d in rounds[0]}
    if len(rounds) > 1:
        greet(known_sem.at[0])
    loaded(w_in)
    w_arrival = [send_weights(full, rows - full, 0, wr.at[0])]
    if rem:
        w_arrival.append(send_weights(rem, rows - radius, full, wr.at[1]))

    row, col = iota((TILE, lons), 0), iota((TILE, lons), 1)

    def lon_matrix(c_hi, c_lo, sign):
        off = sign * (col - row) + radius
        off = jnp.where(off < 0, off + lons, off)
        off = jnp.where(off >= lons, off - lons, off)
        base = jnp.zeros((TILE, lons), F32)
        for j in range(width):
            base = jnp.where(off == j, lon_t[j], base)
        for i in range(0, lons, PACK):
            value = jnp.concatenate(
                [pltpu.roll(base, i, 1) if i else base, pltpu.roll(base, i + TILE, 1)], axis=0
            )
            c_hi[i:i + PACK], c_lo[i:i + PACK] = split(value)

    lon_matrix(a_hi, a_lo, 1)
    level_of = [
        order[source(q // own_levels) * own_levels + q % own_levels] for q in range(levels)
    ]
    loaded(p_in)

    def scaled(q):
        for v in range(2):
            for k in range(members):
                pf_ref[q, v, k * rows:(k + 1) * rows] = p_ref[k, v, level_of[q]].astype(F32) * norm

    z_arrival = {}
    ordered = [d * own_levels + j for d in arrival for j in range(own_levels)]
    parts = math.gcd(PARTS, members)
    unfiltered = ordered[own_levels:min(2 * own_levels, levels - 1)]

    def send_level(q):
        d, j = divmod(q, own_levels)
        g0 = jnp.concatenate([g_all[d, 0, j]] * members, axis=0)
        g1 = jnp.concatenate([g_all[d, 1, j]] * members, axis=0)
        x = pf_ref[q, 0] * g0 + pf_ref[q, 1] * g1
        src = z_ref.at[q]
        if q in unfiltered:
            src = x_ref.at[j]
            x_ref[j] = x
        else:
            z_ref[q] = filter_lon(x, a_hi, a_lo)
        size = stack // parts if q == ordered[-1] else stack
        z_arrival[q] = [
            to_bands(
                far_then_near,
                lambda side, at=at: (src.at[at:at + size], zn_ref.at[side, q, at:at + size]),
                lambda count, at=at: zn_ref.at[0:count, q, at:at + size],
                zr.at[levels + i - 1 if i else q],
            )
            for i, at in enumerate(range(0, stack, size))
        ]
        if q in unfiltered:
            z_ref[q] = filter_lon(x, a_hi, a_lo)

    early = len(sent)
    for j in range(own_levels):
        scaled(j)
        send_level(j)
    loaded(lev_in)
    loaded(lat_in)
    for i in range(1, len(rounds)):
        pl.semaphore_wait(known_sem.at[i - 1], len(direct))
        if i + 1 < len(rounds):
            greet(known_sem.at[i])
        gathers.update({d: gather(d) for d in rounds[i]})

    for q in range(own_levels, levels):
        scaled(q)
    for side, present in ((0, has_low), (1, has_high)):
        @pl.when(jnp.logical_not(present))
        def _():
            for q in range(levels):
                zn_ref[side, q] = jnp.zeros((stack, lons), F32)
            wn_ref[side] = jnp.zeros(wn_ref.shape[1:], F32)

    lon_matrix(b_hi, b_lo, -1)

    def thirds(shape):
        c, size = iota(shape, 1), shape[1] // 3
        third = (c >= size).astype(jnp.int32) + (c >= 2 * size).astype(jnp.int32)
        return third, c - third * size

    def halo_pos(h):
        s = h - 2 * full
        rest = jnp.where(s < rem, rows + full + s, s - full - TILE)
        rest = jnp.where((s >= rem) & (s < TILE - rem), -4 * rows, rest)
        return jnp.where(h < full, h - full, jnp.where(h < 2 * full, rows + h - full, rest))

    def lat_matrix(out_pos, in_pos, third, sign):
        shift = sign * (in_pos - out_pos)
        value = jnp.zeros(shift.shape, F32)
        for j in range(width):
            value = jnp.where(shift == j - radius, lat_t[j], value)
        high = value.astype(BF16).astype(F32)
        return jnp.where(third == 1, value - high, high).astype(BF16)

    far = 8 * rows
    for k_ref, is_own in ((k_own, True), (k_halo, False)):
        r = iota(k_ref.shape, 0)
        third, c = thirds(k_ref.shape)
        if is_own:
            in_pos = jnp.where(c < rows, c, far)
        else:
            in_pos = jnp.where(c < rows, c - rows, jnp.where(c < 2 * rows, c, far))
        out_pos = jnp.where(r < rows, r, halo_pos(r - rows))
        k_ref[...] = lat_matrix(out_pos, in_pos, third, -1)
    third, c = thirds(k_fwd.shape)
    in_pos = jnp.where(c < rows, c, halo_pos(c - rows))
    inside = (in_pos + band * rows >= 0) & (in_pos + band * rows < bands * rows)
    inside = inside & (c < rows + halo)
    k_fwd[...] = lat_matrix(iota(k_fwd.shape, 0), jnp.where(inside, in_pos, far), third, 1)

    coef = []
    for l in range(levels):
        coef.append([])
        for q in range(levels):
            tap = l - level_of[q] + lev_width // 2
            inside = (tap >= 0) & (tap < lev_width)
            value = lev_t[jnp.clip(tap, 0, lev_width - 1)]
            coef[l].append(jnp.where(inside, value, 0.0))

    for d in arrival[1:]:
        if d == arrival[2]:
            settle(keep=len(sent) - early)
        gathers[d].wait_recv()
        for j in range(own_levels):
            send_level(d * own_levels + j)

    for wait in w_arrival:
        wait()
    s = iota((TILE, lons), 0)
    for k in range(members):
        at = slice(k * rows, (k + 1) * rows)
        for l in range(levels):
            wh_ref[k, l, 0:full] = wn_ref[0, k, l, edge - full:edge]
            wh_ref[k, l, full:2 * full] = wn_ref[1, k, l, 0:full]
            if rem:
                wh_ref[k, l, 2 * full:halo] = jnp.where(
                    s < rem, wn_ref[1, k, l, full:edge], wn_ref[0, k, l, 0:TILE]
                )
        own = [dot(k_own[...], stacked(z_ref[q, at])) for q in range(levels)]
        for l in range(levels):
            total = jnp.concatenate([w_ref[k, l], wh_ref[k, l]], axis=0)
            for q in range(levels):
                total = total + coef[l][q] * own[q]
            acc_ref[k, l] = total

    for q in ordered[:-1]:
        z_arrival[q][0]()
        if q in unfiltered:
            z = filter_lon(jnp.concatenate([zn_ref[0, q], zn_ref[1, q]], axis=0), a_hi, a_lo)
            zn_ref[0, q], zn_ref[1, q] = z[:stack], z[stack:]
        for k in range(members):
            at = slice(k * rows, (k + 1) * rows)
            y = dot(k_halo[...], stacked(jnp.concatenate([zn_ref[0, q, at], zn_ref[1, q, at]], axis=0)))
            for l in range(levels):
                acc_ref[k, l] = acc_ref[k, l] + coef[l][q] * y

    settle(keep=parts)
    q = ordered[-1]
    backward = arrival[::-1]
    outgoing = [d * own_levels + j for d in backward[:-1] for j in range(own_levels)]
    part = stack // parts

    def filtered_part(g):
        at = slice(g * part, (g + 1) * part)
        high = jnp.concatenate([f_hi[j, at] for j in outgoing], axis=0)
        low = jnp.concatenate([f_lo[j, at] for j in outgoing], axis=0)
        return filter_split(high, low, b_hi, b_lo)

    for i in range(parts):
        z_arrival[q][i]()
        group = range(i * members // parts, (i + 1) * members // parts)
        last = {}
        for k in group:
            at = slice(k * rows, (k + 1) * rows)
            x = jnp.concatenate([zn_ref[0, q, at], zn_ref[1, q, at]], axis=0)
            last[k] = dot(k_halo[...], stacked(x))
        if i == parts - 1:
            filtered = [filtered_part(g) for g in range(i)]
        fields = {j: [] for j in range(levels)}
        for k in group:
            y = []
            for l in range(levels):
                w = jnp.concatenate([w_ref[k, l], wh_ref[k, l]], axis=0)
                total = acc_ref[k, l] + coef[l][q] * last[k]
                u = w - STEP_RATE * total / (1.0 + jnp.abs(total))
                u_ref[k, l] = u[0:rows]
                y.append(dot(k_fwd[...], stacked(u)))
            for j in range(levels):
                field = coef[0][j] * y[0]
                for l in range(1, levels):
                    field = field + coef[l][j] * y[l]
                fields[j].append(field)
        at = slice(group[0] * rows, (group[-1] + 1) * rows)
        for j in range(levels):
            f_hi[j, at], f_lo[j, at] = split(jnp.concatenate(fields[j], axis=0))

    scatter_sem = free.pop(0)
    filtered.append(filtered_part(parts - 1))

    def increment(q, fields):
        for v in range(2):
            inc = None
            for g, field in enumerate(fields):
                terms = pf_ref[q, v, g * field.shape[0]:(g + 1) * field.shape[0]] * field
                for k in range(0, field.shape[0], rows):
                    term = terms[k:k + rows]
                    inc = term if inc is None else inc + term
            inc_ref[q // own_levels, v, q % own_levels] = inc

    for i, q in enumerate(outgoing):
        increment(q, [f[i * part:(i + 1) * part] for f in filtered])
        d = q // own_levels
        if (q + 1) % own_levels == 0:
            remote(inc_ref.at[d], rs_ref.at[d - 1], rsr, scatter_sem, (source(d), band)).start()
    for q in range(own_levels):
        increment(q, [filter_split(f_hi[q], f_lo[q], b_hi, b_lo)])
    settle()
    pltpu.make_async_copy(rs_ref, rs_ref, rsr).wait()
    result = inc_ref[0]
    for d in range(1, n):
        result = result + rs_ref[d - 1]
    out_ref[...] = result
    pltpu.make_async_copy(rs_ref, rs_ref, pool.at[scatter_sem]).wait()


def write_out(u_ref, inc_ref, upd_hbm, inc_hbm, sem):
    first = pltpu.make_async_copy(u_ref, upd_hbm, sem.at[0])
    second = pltpu.make_async_copy(inc_ref, inc_hbm, sem.at[1])
    first.start()
    second.start()
    first.wait()
    second.wait()


def on_device(gradient, perturbations, weights, lon_taps, lat_taps, lev_taps, level_order):
    n, bands = lax.axis_size("mem"), lax.axis_size("lat")
    members, levels, rows, lons = weights.shape
    radius = lat_taps.shape[0] // 2
    norm = 1.0 / math.sqrt(members * n - 1)
    full, rem, halo, edge = sizes(rows, radius)
    stack = members * rows
    vmem, dma = pltpu.VMEM, pltpu.SemaphoreType.DMA
    anywhere = pl.BlockSpec(memory_space=pl.ANY)
    in_vmem = pl.BlockSpec(memory_space=pltpu.VMEM)
    updated, increment = pl.pallas_call(
        functools.partial(kernel, n, bands, norm, radius, lev_taps.shape[0]),
        out_shape=(
            vmem(weights.shape, F32),
            vmem(gradient.shape, F32),
        ),
        in_specs=[anywhere] * 7,
        out_specs=(in_vmem, in_vmem),
        scratch_shapes=[
            vmem((n,) + gradient.shape, F32),
            vmem(perturbations.shape, BF16),
            vmem((levels, 2, stack, lons), F32),
            vmem(weights.shape, F32),
            vmem((2, members, levels, edge, lons), F32),
            vmem((members, levels, halo, lons), F32),
            vmem((gradient.shape[1], stack, lons), F32),
            vmem((levels, stack, lons), F32),
            vmem((2, levels, stack, lons), F32),
            vmem((members, levels, rows + halo, lons), F32),
            vmem((levels, stack, lons), BF16),
            vmem((levels, stack, lons), BF16),
            vmem((n,) + gradient.shape, F32),
            vmem((n - 1,) + gradient.shape, F32),
            vmem((lons, lons), BF16),
            vmem((lons, lons), BF16),
            vmem((lons, lons), BF16),
            vmem((lons, lons), BF16),
            vmem((rows + halo, 3 * packed(rows)), BF16),
            vmem((rows + halo, 3 * packed(2 * rows)), BF16),
            vmem((rows, 3 * packed(rows + halo)), BF16),
            pltpu.SMEM(lon_taps.shape, F32),
            pltpu.SMEM(lat_taps.shape, F32),
            pltpu.SMEM(lev_taps.shape, F32),
            pltpu.SMEM(level_order.shape, jnp.int32),
            dma((max(7, n + levels - 1),)),
            pltpu.SemaphoreType.REGULAR((max(1, n.bit_length() - 2),)),
            dma((n - 1,)),
            dma((levels + math.gcd(PARTS, members) - 1,)),
            dma((2,)),
            dma,
        ],
        compiler_params=pltpu.CompilerParams(collective_id=0, has_side_effects=True),
        name="step",
    )(gradient, perturbations, weights, lon_taps, lat_taps, lev_taps, level_order)
    return pl.pallas_call(
        write_out,
        out_shape=(
            jax.ShapeDtypeStruct(updated.shape, F32),
            jax.ShapeDtypeStruct(increment.shape, F32),
        ),
        in_specs=[in_vmem] * 2,
        out_specs=(anywhere, anywhere),
        scratch_shapes=[dma((2,))],
        name="write_out",
    )(
        pltpu.with_memory_space_constraint(updated, pltpu.VMEM),
        pltpu.with_memory_space_constraint(increment, pltpu.VMEM),
    )


def solution(mesh):
    in_specs = (
        P(None, "mem", "lat", None),
        P("mem", None, None, "lat", None),
        P("mem", None, "lat", None),
        P(),
        P(),
        P(),
        P(),
    )
    out_specs = (P("mem", None, "lat", None), P(None, "mem", "lat", None))
    return jax.shard_map(
        on_device, mesh=mesh, in_specs=in_specs, out_specs=out_specs, check_vma=False
    )
```
